32 devices in a mesh: ctx: 4 (over y, core), exp: 8 (over z, x).
Axes of the slice: x: 2, y: 2, z: 4, core: 2. Of those that a mesh axis runs over, the one named last changes fastest.
Arguments:
- layer_input: bfloat16 [8, 1536, 2048], P('exp', 'ctx'), may hold values from -30 to 30
- block_ids: int32 [8, 8], P('exp'), may hold values from 0 to 7, as said below
- routes: int32 [8, 1536, 8], P('exp', 'ctx'), may hold values from 0 to 15, all different within a row
- w_query: bfloat16 [2048, 2048], P('exp'), may hold values from -0.125 to 0.125
- w_key: bfloat16 [2048, 2048], P('exp'), may hold values from -0.125 to 0.125
- w_value: bfloat16 [2048, 2048], P('exp'), may hold values from -0.125 to 0.125
- w_output: bfloat16 [2048, 2048], P('exp'), may hold values from -2 to 2
- w_router: bfloat16 [2048, 16], P('exp'), may hold values from -0.0625 to 0.0625
- norm_gains: bfloat16 [2048, 4], P('exp'), may hold values from 0.25 to 1.75
- w_gate_up: bfloat16 [16, 4096, 1024], P('exp', None, 'ctx'), may hold values from -0.125 to 0.125
- w_down: bfloat16 [16, 2048, 1024], P('exp', None, 'ctx'), may hold values from -4 to 4
- d_out: bfloat16 [8, 1536, 2048], P('exp', 'ctx'), may hold values from -6 to 6
Outputs:
- output: bfloat16 [8, 1536, 2048], P('exp', 'ctx')
- d_x: float32 [8, 1536, 2048], P('exp', 'ctx')
- g_query: float32 [2048, 2048], P('exp')
- g_key: float32 [2048, 2048], P('exp')
- g_value: float32 [2048, 2048], P('exp')
- g_output: float32 [2048, 2048], P('exp')
- g_router: float32 [2048, 16], P('exp')
- g_gains: float32 [2048, 4], P('exp')
- g_gate_up: float32 [16, 4096, 1024], P('exp', None, 'ctx')
- g_down: float32 [16, 2048, 1024], P('exp', None, 'ctx')
The draws below stay inside these ranges and needn't reach their ends.
Inputs may be any that keep to these rules, and one draw needn't show every extreme that they name: `block_ids`: each row holds each block number once; the two blocks of one device add up to 7. `routes`: each token names 8 different experts.
All inputs are finite; a program needn't handle non-finite values.
Results may differ from the reference program's by a relative error of at most 0.025.
Values may be sent and summed in bfloat16 or wider, within the bound.
A program may use at most 448 MiB of HBM per device.

```python
import math
import jax
import jax.numpy as jnp
from jax import lax

D = 2048
HEADS = 16
HEAD_DIM = 128
FF = 1024
TOP = 8
SEQ_LEN = 1536
EXPERTS = 16
SEQS = 8
TOK_DEV = 384
HALF = 192
BLOCKS = 8
CAP = 240
N_CTX = 4


def draw_layer_input(key, part):
    base_key = jax.random.fold_in(key, 101)
    row_key = jax.random.fold_in(key, 102)
    column_key = jax.random.fold_in(key, 103)
    base = jnp.clip(jax.random.normal(base_key, (SEQS, SEQ_LEN, D), jnp.float32), -4.0, 4.0)
    row_scale = jnp.exp(jax.random.uniform(row_key, (SEQS, SEQ_LEN, 1), jnp.float32, math.log(0.25), math.log(2.5)))
    column_scale = jnp.exp(jax.random.uniform(column_key, (1, 1, D), jnp.float32, math.log(0.3), math.log(3.0)))
    return (base * row_scale * column_scale).astype(jnp.bfloat16)


def draw_block_ids(key, part):
    pair_count = BLOCKS // 2
    perm_keys = jax.random.split(jax.random.fold_in(key, 11), SEQS)

    def one_row(row_key):
        return jax.random.permutation(row_key, pair_count)
    lower_blocks = jax.vmap(one_row)(perm_keys).astype(jnp.int32)
    flips = jax.random.randint(jax.random.fold_in(key, 12), (SEQS, pair_count), 0, 2, dtype=jnp.int32)
    upper_blocks = (BLOCKS - 1 - lower_blocks).astype(jnp.int32)
    first_block = jnp.where(flips == 1, upper_blocks, lower_blocks)
    second_block = jnp.where(flips == 1, lower_blocks, upper_blocks)
    return jnp.stack([first_block, second_block], axis=2).reshape(SEQS, BLOCKS).astype(jnp.int32)


def block_scale(stream_key, shape, shards, least, largest):
    def one(axis_at, parts):
        steps = jax.random.uniform(jax.random.fold_in(jax.random.fold_in(stream_key, 6), axis_at), (parts,), jnp.float32, least / len(shards), largest / len(shards))
        return jnp.repeat(jnp.exp(steps), shape[axis_at] // parts).reshape((-1,) + (1,) * (len(shape) - axis_at - 1))

    factor_of = one(*shards[0])
    for cut in shards[1:]:
        factor_of = factor_of * one(*cut)
    return factor_of


def picks_of(stream_key, rows, number_of, top, lift):
    sequence = jax.random.permutation(jax.random.fold_in(stream_key, 1), number_of)
    favour = sequence
    for power in range(3):
        favour = favour * favour // number_of
    favour = favour * lift // number_of
    lots = jax.random.randint(jax.random.fold_in(stream_key, 2), (rows, number_of), 0, 4096) + favour
    holders = jax.random.permutation(jax.random.fold_in(stream_key, 3), rows)[jnp.arange(number_of) % rows]
    lots = jnp.where(jnp.arange(rows)[:, None] == holders[None, :], 1 << 14, lots)
    score = lots * number_of + jnp.arange(number_of)
    return lax.top_k(score.astype(jnp.int32), top)[1].astype(jnp.int32)


def scatter_about(rng, dims, width, reach, pieces=(), kind=jnp.bfloat16):
    entries = jax.random.normal(rng, dims, jnp.float32) * width
    if len(pieces) > 0:
        entries = block_scale(rng, dims, pieces, -0.22, 0.18) * entries
    return jnp.clip(entries, min=-reach, max=reach).astype(kind)


def setup_inputs(seed: int = 0) -> dict:
    streams_of = jax.random.split(jax.random.key(seed), 13)
    layer_input = draw_layer_input(jax.random.fold_in(streams_of[12], 71), 0)
    block_ids = draw_block_ids(jax.random.fold_in(streams_of[12], 71), 0)
    routes = picks_of(streams_of[2], SEQS * SEQ_LEN, EXPERTS, TOP, 4096).reshape((SEQS, SEQ_LEN, TOP))
    w_query = scatter_about(streams_of[3], (D, D), D ** -0.5, 0.125, ((0, 8),))
    w_key = scatter_about(streams_of[4], (D, D), D ** -0.5, 0.125, ((0, 8),))
    w_value = scatter_about(streams_of[5], (D, D), D ** -0.5, 0.125, ((0, 8),))
    w_output = scatter_about(streams_of[6], (D, D), (max(D // 256, 4)) ** -0.5, 2.0, ((0, 8),))
    w_router = scatter_about(streams_of[7], (D, EXPERTS), (4 * D) ** -0.5, 0.0625, ((0, 8),))
    norm_gains = jnp.clip(1.0 + 0.15 * jax.random.normal(streams_of[8], (D, 4), jnp.float32), 0.25, 1.75).astype(jnp.bfloat16)
    w_gate_up = scatter_about(streams_of[9], (EXPERTS, 2 * D, FF), D ** -0.5, 0.125, ((0, 8), (2, 4)))
    w_down = scatter_about(streams_of[10], (EXPERTS, D, FF), 0.6, 4.0, ((0, 8), (2, 4)))
    d_out = scatter_about(streams_of[11], (SEQS, SEQ_LEN, D), 1.0, 6.0, ((0, 8), (1, 4)))
    return {"layer_input": layer_input, "block_ids": block_ids, "routes": routes, "w_query": w_query, "w_key": w_key, "w_value": w_value, "w_output": w_output, "w_router": w_router, "norm_gains": norm_gains, "w_gate_up": w_gate_up, "w_down": w_down, "d_out": d_out}


epsilon = 1e-05
rope_theta = 10000.0

@jax.custom_vjp
def low(v):
    return lax.optimization_barrier(v.astype(jnp.bfloat16)).astype(jnp.float32)

@jax.custom_vjp
def low_back(v):
    return v

def low_keep(v):
    return (low(v), None)

def low_pass(kept, grad):
    return (grad,)

def back_keep(v):
    return (v, None)

def back_low(kept, grad):
    return (low(grad),)
low.defvjp(low_keep, low_pass)
low_back.defvjp(back_keep, back_low)

def matmul_high(left, right):
    return jnp.dot(left, right, precision=lax.Precision.HIGHEST)

def rms_scale(matrix, gain):
    return matrix * lax.rsqrt(lax.optimization_barrier(jnp.mean(matrix * matrix, axis=-1, keepdims=True)) + epsilon) * gain

def angle_tables(positions, head_width):
    half_width = head_width // 2
    inverse = rope_theta ** (-(jnp.arange(half_width, dtype=jnp.float32) * 2.0) / head_width)
    angles = positions.astype(jnp.float32)[:, None] * inverse[None, :]
    angles = jnp.concatenate([angles, angles], axis=-1)
    return (jnp.cos(angles), jnp.sin(angles))

def rotate(matrix, cosine, sine, head_count, head_width):
    row_count = matrix.shape[0]
    split_heads = matrix.reshape(row_count, head_count, head_width)
    half_width = head_width // 2
    turned = jnp.concatenate([-split_heads[..., half_width:], split_heads[..., :half_width]], axis=-1)
    result = split_heads * cosine[:, None, :] + turned * sine[:, None, :]
    return result.reshape(row_count, head_count * head_width)

def all_positions(block_row, half_rows):
    offsets = jnp.arange(half_rows, dtype=jnp.int32)
    return (block_row[:, None] * half_rows + offsets[None, :]).reshape(-1).astype(jnp.int32)

def slot_table(route_rows, expert_count, capacity):
    flat_routes = route_rows.reshape(-1)
    onehot = (flat_routes[:, None] == jnp.arange(expert_count, dtype=jnp.int32)[None, :]).astype(jnp.int32)
    rank_of = lax.optimization_barrier(jnp.sum(jnp.cumsum(onehot, axis=0) * onehot, axis=1)) - 1
    kept_mask = rank_of < capacity
    pair_slot = jnp.where(kept_mask, flat_routes * capacity + rank_of, expert_count * capacity)
    return (pair_slot.astype(jnp.int32), kept_mask)

def forward(tokens, w_query, w_key, w_value, w_output, w_router, norm_gains, w_gate_up, w_down, block_ids, routes):
    score_scale = HEAD_DIM ** (-0.5)

    def expert_block(packed):
        normed_dev, probs_dev, routes_dev = packed
        pair_slot, kept_mask = slot_table(routes_dev, EXPERTS, CAP)
        pair_rows = jnp.repeat(normed_dev, TOP, axis=0)
        buffer = jnp.zeros((EXPERTS * CAP + 1, D), jnp.float32).at[pair_slot].set(pair_rows)
        arrived = low_back(buffer[:EXPERTS * CAP].reshape(EXPERTS, CAP, D))
        gate_pre = low_back(jnp.einsum('ecd,edf->ecf', arrived, w_gate_up[:, :D], precision=lax.Precision.HIGHEST))
        up_pre = low_back(jnp.einsum('ecd,edf->ecf', arrived, w_gate_up[:, D:], precision=lax.Precision.HIGHEST))
        inner = low(jax.nn.silu(gate_pre) * up_pre)
        expert_out = low(low_back(jnp.einsum('ecf,edf->ecd', inner, w_down, precision=lax.Precision.HIGHEST)))
        padded = jnp.concatenate([expert_out.reshape(EXPERTS * CAP, D), jnp.zeros((1, D), jnp.float32)], axis=0)
        pair_out = padded[pair_slot].reshape(TOK_DEV, TOP, D)
        chosen_mask = (routes_dev[..., None] == jnp.arange(EXPERTS, dtype=jnp.int32)[None, None, :]).astype(jnp.float32)
        gates = lax.optimization_barrier(jnp.sum(chosen_mask * probs_dev[:, None, :], axis=-1))
        return lax.optimization_barrier(jnp.sum(gates[..., None] * pair_out, axis=1))

    def one_sequence(packed):
        seq_tokens, seq_blocks, seq_routes = packed
        positions = all_positions(seq_blocks, HALF)
        cosine, sine = angle_tables(positions, HEAD_DIM)
        first_norm = low(rms_scale(seq_tokens, norm_gains[:, 0]))
        query = low(rotate(rms_scale(low_back(matmul_high(first_norm, w_query)), norm_gains[:, 1]), cosine, sine, HEADS, HEAD_DIM))
        keys = low(rotate(rms_scale(low_back(matmul_high(first_norm, w_key)), norm_gains[:, 2]), cosine, sine, HEADS, HEAD_DIM))
        values = low(low_back(matmul_high(first_norm, w_value)))
        query_heads = query.reshape(SEQ_LEN, HEADS, HEAD_DIM)
        key_heads = keys.reshape(SEQ_LEN, HEADS, HEAD_DIM)
        value_heads = values.reshape(SEQ_LEN, HEADS, HEAD_DIM)
        scores = low_back(jnp.einsum('qhd,khd->hqk', query_heads, key_heads, precision=lax.Precision.HIGHEST) * score_scale)
        visible = positions[None, :] <= positions[:, None]
        scores = jnp.where(visible[None], scores, -1e+30)
        probs = jax.nn.softmax(scores, axis=-1)
        attended = jnp.einsum('hqk,khd->qhd', low(probs), value_heads, precision=lax.Precision.HIGHEST).reshape(SEQ_LEN, D)
        branch = low_back(matmul_high(low(low_back(attended)), w_output))
        hidden = seq_tokens + branch
        second_norm = low(rms_scale(hidden, norm_gains[:, 3]))
        logits = low_back(matmul_high(second_norm, w_router))
        router_probs = jax.nn.softmax(logits, axis=-1)
        mixture = lax.map(jax.checkpoint(expert_block), (second_norm.reshape(N_CTX, TOK_DEV, D), router_probs.reshape(N_CTX, TOK_DEV, EXPERTS), seq_routes.reshape(N_CTX, TOK_DEV, TOP)))
        return hidden + mixture.reshape(SEQ_LEN, D)
    return lax.map(jax.checkpoint(one_sequence), (tokens, block_ids, routes))

def reference(layer_input, block_ids, routes, w_query, w_key, w_value, w_output, w_router, norm_gains, w_gate_up, w_down, d_out):
    floats = (layer_input.astype(jnp.float32), w_query.astype(jnp.float32), w_key.astype(jnp.float32), w_value.astype(jnp.float32), w_output.astype(jnp.float32), w_router.astype(jnp.float32), norm_gains.astype(jnp.float32), w_gate_up.astype(jnp.float32), w_down.astype(jnp.float32))

    def forward_of(tokens, query_w, key_w, value_w, output_w, router_w, gain_table, gate_up_w, down_w):
        return forward(tokens, query_w, key_w, value_w, output_w, router_w, gain_table, gate_up_w, down_w, block_ids, routes)
    result, pullback = jax.vjp(forward_of, *floats)
    grads = pullback(d_out.astype(jnp.float32))
    return (result.astype(jnp.bfloat16), grads[0], grads[1], grads[2], grads[3], grads[4], grads[5], grads[6], grads[7], grads[8])
```

```python
import functools

import jax
import jax.numpy as jnp
from jax import lax
from jax.experimental import pallas as pl
from jax.experimental.pallas import tpu as pltpu
from jax.sharding import PartitionSpec as P

HEAD_DIM = 128
CORES = 2
ROWS_Z = 4

epsilon = 1e-05
rope_theta = 10000.0
BF = jnp.bfloat16
F32 = jnp.float32


def dot(a, b, dims):
    return lax.dot_general(a, b, (dims, ((), ())), preferred_element_type=F32)


def ring_order(count):
    rows = ROWS_Z if count % ROWS_Z == 0 else 1
    across = count // rows
    walk = [(0, 0)]
    for z in range(rows):
        xs = range(1, across)
        walk += [(z, x) for x in (xs if z % 2 == 0 else reversed(xs))]
    walk += [(z, 0) for z in range(rows - 1, 0, -1)]
    return [z * across + x for z, x in walk]


class Ring:
    def __init__(self, axis, rings):
        self.axis = axis
        self.size = len(rings[0])
        self.right = [
            (r[i], r[(i + 1) % self.size]) for r in rings for i in range(self.size)
        ]
        self.left = [(b, a) for a, b in self.right]

    def go_right(self, v):
        return lax.ppermute(v, self.axis, self.right)

    def go_left(self, v):
        return lax.ppermute(v, self.axis, self.left)

    def gather(self, v):
        n = self.size
        got = [None] * n
        got[0] = v
        right = left = v
        for s in range(1, n // 2):
            right = self.go_right(right)
            left = self.go_left(left)
            got[s], got[n - s] = right, left
        half = v.shape[0] // 2
        got[n // 2] = jnp.concatenate(
            [self.go_right(right[:half]), self.go_left(left[half:])], axis=0
        )
        return got

    def scatter(self, part, dtype=BF):
        n = self.size
        far = part(n // 2).astype(dtype)
        half = far.shape[0] // 2
        from_left = self.go_right(far[:half]).astype(F32)
        from_right = self.go_left(far[half:]).astype(F32)
        from_left = jnp.concatenate([from_left, jnp.zeros_like(from_left)], axis=0)
        from_right = jnp.concatenate([jnp.zeros_like(from_right), from_right], axis=0)
        for s in range(n // 2 - 1, 0, -1):
            to_right = (part(s) + from_left).astype(dtype)
            to_left = (part(n - s) + from_right).astype(dtype)
            from_left = self.go_right(to_right).astype(F32)
            from_right = self.go_left(to_left).astype(F32)
        return part(0) + from_left + from_right


def _sorted_copy(dst, src, place, half, blocks):
    for b in range(blocks):
        at = pl.multiple_of(place[b] * half, half)
        dst[b * half : (b + 1) * half, :] = src[pl.ds(at, half), :]


def _scores(q, k, row0, width, scale):
    raw = dot(q, k, (((1,), (1,)))) * scale
    rows = lax.broadcasted_iota(jnp.int32, raw.shape, 0) + row0
    cols = lax.broadcasted_iota(jnp.int32, raw.shape, 1)
    return jnp.where(cols <= rows, raw, -1e30)


def _attend_kernel(place, q_ref, k_ref, v_ref, o_ref, lse_ref, q_s, k_s, v_s, o_s, *, half, blocks, tile, scale):
    for dst, src in ((q_s, q_ref), (k_s, k_ref), (v_s, v_ref)):
        _sorted_copy(dst, src, place, half, blocks)
    for i in range(half * blocks // tile):
        width = (i + 1) * tile
        s = _scores(q_s[i * tile : width, :], k_s[:width, :], i * tile, width, scale)
        top = jnp.max(s, axis=-1, keepdims=True)
        total = top + jnp.log(jnp.sum(jnp.exp(s - top), axis=-1, keepdims=True))
        p = jnp.exp(s - total).astype(BF)
        o_s[i * tile : width, :] = dot(p, v_s[:width, :], ((1,), (0,))).astype(BF)
        lse_ref[0, i * tile : width, :] = total
    for b in range(blocks):
        at = pl.multiple_of(place[b] * half, half)
        o_ref[pl.ds(at, half), :] = o_s[b * half : (b + 1) * half, :]


def _attend_back_kernel(place, q_ref, k_ref, v_ref, d_ref, lse_ref, dq_ref, dk_ref, dv_ref,
                        q_s, k_s, v_s, d_s, dq_s, dk_s, dv_s, *, half, blocks, tile, scale):
    for dst, src in ((q_s, q_ref), (k_s, k_ref), (v_s, v_ref), (d_s, d_ref)):
        _sorted_copy(dst, src, place, half, blocks)
    count = half * blocks // tile
    for i in reversed(range(count)):
        width = (i + 1) * tile
        here = slice(i * tile, width)
        q, d, k, v = q_s[here, :], d_s[here, :], k_s[:width, :], v_s[:width, :]
        p = jnp.exp(_scores(q, k, i * tile, width, scale) - lse_ref[0, here, :])
        dp = dot(d, v, ((1,), (1,)))
        row = jnp.sum(p * dp, axis=-1, keepdims=True)
        ds = (p * (dp - row)).astype(BF)
        dq_s[here, :] = dot(ds, k, ((1,), (0,))) * scale
        dk = dot(ds, q, ((0,), (0,))) * scale
        dv = dot(p.astype(BF), d, ((0,), (0,)))
        if i == count - 1:
            dk_s[:width, :] = dk
            dv_s[:width, :] = dv
        else:
            dk_s[:width, :] += dk
            dv_s[:width, :] += dv
    for b in range(blocks):
        at = pl.multiple_of(place[b] * half, half)
        for dst, src in ((dq_ref, dq_s), (dk_ref, dk_s), (dv_ref, dv_s)):
            dst[pl.ds(at, half), :] = src[b * half : (b + 1) * half, :].astype(dst.dtype)


def _head_specs(rows):
    head = pl.BlockSpec((rows, HEAD_DIM), lambda h, place: (0, h))
    lse = pl.BlockSpec((1, rows, 1), lambda h, place: (h, 0, 0))
    return head, lse


def attend(place, q, k, v, half):
    rows, width = q.shape
    heads = width // HEAD_DIM
    head, lse = _head_specs(rows)
    body = functools.partial(_attend_kernel, half=half, blocks=rows // half, tile=min(384, rows), scale=HEAD_DIM**-0.5)
    return pl.pallas_call(
        body,
        grid_spec=pltpu.PrefetchScalarGridSpec(
            num_scalar_prefetch=1,
            grid=(heads,),
            in_specs=[head] * 3,
            out_specs=[head, lse],
            scratch_shapes=[pltpu.VMEM((rows, HEAD_DIM), BF)] * 4,
        ),
        out_shape=[
            jax.ShapeDtypeStruct((rows, width), BF),
            jax.ShapeDtypeStruct((heads, rows, 1), F32),
        ],
        compiler_params=pltpu.CompilerParams(vmem_limit_bytes=48 << 20),
        cost_estimate=pl.CostEstimate(flops=2 * rows * rows * width * 2, bytes_accessed=8 * rows * width, transcendentals=heads * rows * rows),
    )(place, q, k, v)


def attend_back(place, q, k, v, d, lse_in, half):
    rows, width = q.shape
    heads = width // HEAD_DIM
    head, lse = _head_specs(rows)
    body = functools.partial(_attend_back_kernel, half=half, blocks=rows // half, tile=min(384, rows), scale=HEAD_DIM**-0.5)
    return pl.pallas_call(
        body,
        grid_spec=pltpu.PrefetchScalarGridSpec(
            num_scalar_prefetch=1,
            grid=(heads,),
            in_specs=[head] * 4 + [lse],
            out_specs=[head] * 3,
            scratch_shapes=[pltpu.VMEM((rows, HEAD_DIM), BF)] * 4
            + [pltpu.VMEM((rows, HEAD_DIM), F32)] * 3,
        ),
        out_shape=[
            jax.ShapeDtypeStruct((rows, width), F32),
            jax.ShapeDtypeStruct((rows, width), F32),
            jax.ShapeDtypeStruct((rows, width), BF),
        ],
        compiler_params=pltpu.CompilerParams(vmem_limit_bytes=48 << 20),
        cost_estimate=pl.CostEstimate(flops=5 * rows * rows * width * 2, bytes_accessed=18 * rows * width, transcendentals=heads * rows * rows),
    )(place, q, k, v, d, lse_in)


def inv_rms(matrix):
    return lax.rsqrt(jnp.mean(matrix * matrix, axis=-1, keepdims=True) + epsilon)


def norm_back(value, gain, grad):
    r = inv_rms(value)
    weighted = gain * grad
    inside = jnp.mean(value * weighted, axis=-1, keepdims=True)
    return r * weighted - value * (r * r * r * inside), jnp.sum(grad * value * r, axis=0)


def angle_tables(positions):
    half_width = HEAD_DIM // 2
    inverse = rope_theta ** (-(jnp.arange(half_width, dtype=F32) * 2.0) / HEAD_DIM)
    angles = positions.astype(F32)[:, None] * inverse[None, :]
    angles = jnp.concatenate([angles, angles], axis=-1)
    return jnp.cos(angles), jnp.sin(angles)


def rope(matrix, cosine, sine, back=False):
    rows, width = matrix.shape
    split = matrix.reshape(rows, width // HEAD_DIM, HEAD_DIM)
    first, second = split[..., : HEAD_DIM // 2], split[..., HEAD_DIM // 2 :]
    turned = [second, -first] if back else [-second, first]
    turned = jnp.concatenate(turned, axis=-1)
    result = split * cosine[:, None, :] + turned * sine[:, None, :]
    return result.reshape(rows, width)


def per_device(
    exp_walk,
    layer_input,
    block_ids,
    routes,
    w_query,
    w_key,
    w_value,
    w_output,
    w_router,
    norm_gains,
    w_gate_up,
    w_down,
    d_out,
):
    C, E = lax.axis_size("ctx"), lax.axis_size("exp")
    c, e = lax.axis_index("ctx"), lax.axis_index("exp")
    Y = C // CORES
    ring = Ring("exp", [exp_walk])
    ctx_ring = Ring("ctx", [[y * CORES + k for y in range(Y)] for k in range(CORES)])
    sibling = [(i, i ^ 1) for i in range(C)]

    def swap(v):
        return lax.ppermute(v, "ctx", sibling)

    def ctx_gather(v):
        got = []
        for block in ctx_ring.gather(v):
            got += [block, swap(block)]
        return got

    def ctx_scatter(part):
        mine = []
        for dy in range(Y):
            sent = swap(part(dy * CORES + 1).astype(BF))
            mine.append(part(dy * CORES) + sent.astype(F32))
        return ctx_ring.scatter(lambda s: mine[(Y - s) % Y])

    def ctx_of(r):
        return lax.rem(c // CORES + Y - r // CORES, Y) * CORES + jnp.bitwise_xor(lax.rem(c, CORES), r % CORES)

    def entry_of(i):
        return lax.rem(c // CORES + Y - i // CORES, Y) * CORES + jnp.bitwise_xor(lax.rem(c, CORES), i % CORES)

    def ctx_sum(rows):
        blocks = rows.reshape(rows.shape[0], C, -1)
        whole = lax.psum(jnp.stack([lax.dynamic_index_in_dim(blocks, entry_of(i), 1, False) for i in range(C)]), "ctx")
        return jnp.concatenate([lax.dynamic_index_in_dim(whole, ctx_of(r), 0, False) for r in range(C)], axis=1)

    walk = jnp.array(exp_walk, jnp.int32)
    place_in_walk = [0] * E
    for i, d in enumerate(exp_walk):
        place_in_walk[d] = i
    my_place = jnp.array(place_in_walk, jnp.int32)[e]
    left_of = [walk[lax.rem(my_place + E - s, E)] for s in range(E)]

    T, D = layer_input.shape[1:]
    rows_e = w_query.shape[0]
    cols_c = D // C
    S = T * C
    half = T // 2
    NE = w_router.shape[1]
    K = routes.shape[2]
    J = w_gate_up.shape[0]
    cap = (5 * T * K + 4 * NE - 1) // (4 * NE)
    x = layer_input[0]
    grad_out = d_out[0]

    x_all = jnp.concatenate(ctx_gather(x), axis=0)

    small = jnp.concatenate(
        [w_router.reshape(-1), norm_gains.reshape(-1), routes.astype(BF).reshape(-1)]
    )
    small_len = small.shape[0]
    small = jnp.pad(small, (0, -small_len % 256)).reshape(-1, 128)
    smalls = [v.reshape(-1) for v in ring.gather(small)]
    cut = rows_e * NE, rows_e * NE + rows_e * norm_gains.shape[1]
    router_full = jnp.zeros((E, rows_e, NE), BF)
    gains_full = jnp.zeros((E, rows_e, norm_gains.shape[1]), BF)
    for s in range(E):
        router_full = lax.dynamic_update_slice(
            router_full, smalls[s][: cut[0]].reshape(1, rows_e, NE), (left_of[s], 0, 0)
        )
        gains_full = lax.dynamic_update_slice(
            gains_full,
            smalls[s][cut[0] : cut[1]].reshape(1, rows_e, -1),
            (left_of[s], 0, 0),
        )
    router_full = router_full.reshape(D, NE)
    gains = gains_full.reshape(D, -1).astype(F32).T
    routes_all = jnp.stack([v[cut[1] : small_len] for v in smalls]).astype(jnp.int32)
    routes_all = routes_all.reshape(E, T, K)

    def my_columns(w):
        return lax.dynamic_slice_in_dim(w, c * cols_c, cols_c, axis=1)

    def assemble(blocks):
        full = jnp.zeros((E * rows_e, blocks[0].shape[1]), BF)
        for s in range(E):
            full = lax.dynamic_update_slice_in_dim(full, blocks[s], left_of[s] * rows_e, axis=0)
        return full

    w_qkv = assemble(ring.gather(jnp.concatenate([my_columns(w) for w in (w_query, w_key, w_value)], axis=1)))
    w_out_cols = assemble(ring.gather(my_columns(w_output)))
    w_out_rows = lax.all_to_all(
        w_out_cols.reshape(C, cols_c, cols_c), "ctx", split_axis=0, concat_axis=0, tiled=True
    )
    w_out_rows = jnp.transpose(w_out_rows, (1, 0, 2)).reshape(cols_c, D)
    w_gu = jnp.concatenate(ctx_gather(w_gate_up), axis=2)
    w_dn = jnp.concatenate(ctx_gather(w_down), axis=2)
    H = w_dn.shape[2]
    shard = H // C
    d_all = ring.gather(grad_out)

    blocks_rel = jnp.stack([lax.dynamic_slice_in_dim(block_ids[0], ctx_of(r) * 2, 2) for r in range(C)]).reshape(-1)
    positions = (blocks_rel[:, None] * half + jnp.arange(half, dtype=jnp.int32)[None, :]).reshape(-1)
    place = jnp.argsort(blocks_rel).astype(jnp.int32)
    cosine, sine = angle_tables(positions)
    gain_q = lax.dynamic_slice_in_dim(gains[1], c * cols_c, cols_c)
    gain_k = lax.dynamic_slice_in_dim(gains[2], c * cols_c, cols_c)

    x_all32 = x_all.astype(F32)
    n1 = (x_all32 * inv_rms(x_all32) * gains[0]).astype(BF)
    qkv = dot(n1, w_qkv, ((1,), (0,)))
    qp, kp = qkv[:, :cols_c], qkv[:, cols_c : 2 * cols_c]
    v = qkv[:, 2 * cols_c :].astype(BF)
    squares = ctx_sum(jnp.stack([jnp.sum(qp * qp, axis=1), jnp.sum(kp * kp, axis=1)]))
    scales = lax.rsqrt(squares / D + epsilon)
    r_q, r_k = scales[0][:, None], scales[1][:, None]
    q = rope(qp * r_q * gain_q, cosine, sine).astype(BF)
    k = rope(kp * r_k * gain_k, cosine, sine).astype(BF)
    attn, lse = attend(place, q, k, v, half)
    branch = dot(attn, w_out_rows, ((1,), (0,)))
    hidden = x.astype(F32) + ctx_scatter(lambda r: branch[r * T : (r + 1) * T])
    n2 = (hidden * inv_rms(hidden) * gains[3]).astype(BF)

    mine = e * J + jnp.arange(J, dtype=jnp.int32)
    chosen = jnp.any(routes_all[:, None] == mine[None, :, None, None], axis=-1)
    before = (jnp.arange(T)[:, None] < jnp.arange(T)[None, :]).astype(BF)
    rank = dot(chosen.astype(BF).reshape(E * J, T), before, ((1,), (0,))).reshape(E, J, T).astype(jnp.int32)
    slot = jnp.where(chosen & (rank < cap), rank, -1)
    pick = (slot[:, :, None, :] == jnp.arange(cap, dtype=jnp.int32)[None, None, :, None]).astype(BF)

    def take(rows):
        return jnp.stack(
            [jnp.einsum("jrt,td->jrd", pick[s], rows[s], preferred_element_type=F32).astype(BF) for s in range(E)], axis=1
        ).reshape(J, E * cap, D)

    xd = take(d_all)
    dw = jnp.einsum("jrd,jdf->jrf", xd, w_dn, preferred_element_type=F32)

    n2_all = ring.gather(n2)
    logits = [dot(n2_all[s], router_full, ((1,), (0,))) for s in range(E)]
    router = [jax.nn.softmax(v, axis=-1) for v in logits]
    is_mine = (jnp.arange(NE, dtype=jnp.int32)[None, :] == mine[:, None]).astype(F32)
    gate = jnp.stack([jnp.sum(router[s][None] * is_mine[:, None, :], axis=-1) for s in range(E)])
    gate_slot = jnp.sum(pick.astype(F32) * gate[:, :, None, :], axis=-1)
    gate_slot = jnp.transpose(gate_slot, (1, 0, 2)).reshape(J, E * cap, 1)
    xin = take(n2_all)
    g = jnp.einsum("jrd,jdf->jrf", xin, w_gu[:, :D], preferred_element_type=F32)
    u = jnp.einsum("jrd,jdf->jrf", xin, w_gu[:, D:], preferred_element_type=F32)
    sig = jax.nn.sigmoid(g)
    act = g * sig
    inner32 = act * u
    inner = inner32.astype(BF)
    dgate_slot = jnp.sum(inner32 * dw, axis=-1).reshape(J, E, cap)
    dinner = gate_slot * dw
    dg = (dinner * u * sig * (1.0 + g * (1.0 - sig))).astype(BF)
    du = (dinner * act).astype(BF)
    inner_gated = (gate_slot * inner32).astype(BF)

    dxin = jnp.einsum("jrf,jdf->jrd", dg, w_gu[:, :D], preferred_element_type=F32)
    dxin = (dxin + jnp.einsum("jrf,jdf->jrd", du, w_gu[:, D:], preferred_element_type=F32)).astype(BF)

    def put(rows):
        rows = rows.reshape(J, E, cap, D)

        def part(s):
            left = (E - s) % E
            return jnp.einsum("jrt,jrd->td", pick[left], rows[:, left], preferred_element_type=F32)

        return part

    dgate = jnp.einsum("sjrt,jsr->sjt", pick.astype(F32), dgate_slot, precision=lax.Precision.HIGHEST)
    dgate_cols = jnp.einsum("sjt,jn->snt", dgate, is_mine, precision=lax.Precision.HIGHEST)
    drouter = ring.scatter(lambda s: dgate_cols[(E - s) % E], F32).T
    router_own = router[0]
    dlogits = (router_own * (drouter - jnp.sum(drouter * router_own, axis=-1, keepdims=True))).astype(BF)
    dn2 = ring.scatter(put(dxin)) + dot(dlogits, router_full, ((1,), (1,)))
    hidden_part, d_gain3 = norm_back(hidden, gains[3], dn2)
    dhidden = grad_out.astype(F32) + hidden_part
    dhidden_all = jnp.concatenate(ctx_gather(dhidden.astype(BF)), axis=0)

    y = jnp.einsum("jrf,jdf->jrd", inner_gated, w_dn, preferred_element_type=F32).astype(BF)
    output = (hidden + ring.scatter(put(y))).astype(BF)[None]

    def weight_grad(rows, cols):
        def part(r):
            return jnp.einsum("jrd,jrf->jdf", rows, cols[..., r * shard : (r + 1) * shard], preferred_element_type=F32)

        return part

    part_g, part_u = weight_grad(xin, dg), weight_grad(xin, du)
    g_gate_up = jnp.concatenate(
        [ctx_scatter(part_g), ctx_scatter(part_u)], axis=1
    )
    g_down = ctx_scatter(weight_grad(xd, inner_gated))

    dattn = dot(dhidden_all, w_out_rows, ((1,), (1,))).astype(BF)
    g_out = dot(attn, dhidden_all, ((0,), (0,))).astype(BF)
    g_out = jnp.transpose(g_out.reshape(cols_c, C, cols_c), (1, 0, 2))
    g_out = lax.all_to_all(g_out, "ctx", split_axis=0, concat_axis=0, tiled=True).reshape(D, cols_c)
    dq, dk, dv = attend_back(place, q, k, v, dattn, lse, half)
    tq, tk = rope(dq, cosine, sine, True), rope(dk, cosine, sine, True)
    wq, wk = tq * gain_q, tk * gain_k
    inside = ctx_sum(jnp.stack([jnp.sum(qp * wq, axis=1), jnp.sum(kp * wk, axis=1)])) / D
    dqp = r_q * wq - qp * (r_q * r_q * r_q * inside[0][:, None])
    dkp = r_k * wk - kp * (r_k * r_k * r_k * inside[1][:, None])
    d_gain1 = jnp.sum(tq * qp * r_q, axis=0)
    d_gain2 = jnp.sum(tk * kp * r_k, axis=0)
    dqkv = jnp.concatenate([dqp.astype(BF), dkp.astype(BF), dv], axis=1)
    dn1_part = dot(dqkv, w_qkv, ((1,), (1,)))
    dn1 = ctx_scatter(lambda r: dn1_part[r * T : (r + 1) * T])
    x32 = x.astype(F32)
    token_part, d_gain0 = norm_back(x32, gains[0], dn1)
    d_x = (dhidden + token_part)[None]

    g_qkv = dot(n1, dqkv, ((0,), (0,))).astype(BF)
    right_of = [walk[lax.rem(my_place + s, E)] for s in range(E)]

    def row_sum(full):
        return ring.scatter(lambda s: lax.dynamic_slice_in_dim(full, right_of[s] * rows_e, rows_e, axis=0).astype(F32))

    g_out_mine = row_sum(g_out)
    g_qkv_mine = row_sum(g_qkv)

    def all_columns(block):
        full = jnp.zeros((rows_e, D), F32)
        for r, piece in enumerate(ctx_gather(block.astype(BF))):
            full = lax.dynamic_update_slice_in_dim(full, piece.astype(F32), ctx_of(r) * cols_c, axis=1)
        return full

    g_query, g_key, g_value = (all_columns(g_qkv_mine[:, i * cols_c : (i + 1) * cols_c]) for i in range(3))
    g_output = all_columns(g_out_mine)

    g_router = dot(n2, dlogits, ((0,), (0,)))
    spread = jnp.zeros((2, D), F32)
    spread = lax.dynamic_update_slice(spread, jnp.stack([d_gain1, d_gain2]), (0, c * cols_c))
    g_small = jnp.concatenate([g_router.T, d_gain0[None], spread, d_gain3[None]], axis=0)
    g_small = lax.psum(g_small, ("ctx", "exp"))
    g_small = lax.dynamic_slice_in_dim(g_small, e * rows_e, rows_e, axis=1).T
    return (
        output,
        d_x,
        g_query,
        g_key,
        g_value,
        g_output,
        g_small[:, :NE],
        g_small[:, NE:],
        g_gate_up,
        g_down,
    )


def solution(mesh):
    exp_walk = ring_order(mesh.shape["exp"])
    tokens = P("exp", "ctx", None)
    rows = P("exp", None)
    hidden_units = P("exp", None, "ctx")
    in_specs = (tokens, rows, tokens) + (rows,) * 6 + (hidden_units, hidden_units, tokens)
    out_specs = (tokens, tokens) + (rows,) * 6 + (hidden_units, hidden_units)
    return jax.shard_map(
        functools.partial(per_device, exp_walk),
        mesh=mesh,
        in_specs=in_specs,
        out_specs=out_specs,
        check_vma=False,
    )
```

```python
import functools

import jax
import jax.numpy as jnp
from jax import lax
from jax.experimental import pallas as pl
from jax.experimental.pallas import tpu as pltpu
from jax.sharding import PartitionSpec as P

HEAD_DIM = 128
CORES = 2
ROWS_Z = 4
VMEM_BYTES = 56 << 20

epsilon = 1e-05
rope_theta = 10000.0
BF = jnp.bfloat16
F32 = jnp.float32


def dot(a, b, dims):
    return lax.dot_general(a, b, (dims, ((), ())), preferred_element_type=F32)


def after(v, *others):
    return lax.optimization_barrier((v, *others))[0]


def zero_of(*arrays):
    return sum(a[(0,) * a.ndim].astype(F32) for a in arrays) * 0.0


def ring_order(count):
    rows = ROWS_Z if count % ROWS_Z == 0 else 1
    across = count // rows
    walk = [(0, 0)]
    for z in range(rows):
        xs = range(1, across)
        walk += [(z, x) for x in (xs if z % 2 == 0 else reversed(xs))]
    walk += [(z, 0) for z in range(rows - 1, 0, -1)]
    return [z * across + x for z, x in walk]


class Ring:
    def __init__(self, axis, rings):
        self.axis = axis
        self.size = len(rings[0])
        self.right = [
            (r[i], r[(i + 1) % self.size]) for r in rings for i in range(self.size)
        ]
        self.left = [(b, a) for a, b in self.right]

    def go_right(self, v):
        return lax.ppermute(v, self.axis, self.right)

    def go_left(self, v):
        return lax.ppermute(v, self.axis, self.left)

    def gather(self, v):
        if self.size == 2:
            return [v, self.go_right(v)]
        walk = Gather(self, v)
        for _ in range(self.size // 2):
            walk.hop()
        return walk.got

    def scatter(self, part, dtype=BF):
        n = self.size
        far = part(n // 2).astype(dtype)
        if n == 2:
            return part(0) + self.go_right(far).astype(F32)
        half = far.shape[0] // 2
        from_left = self.go_right(far[:half]).astype(F32)
        from_right = self.go_left(far[half:]).astype(F32)
        from_left = jnp.concatenate([from_left, jnp.zeros_like(from_left)], axis=0)
        from_right = jnp.concatenate([jnp.zeros_like(from_right), from_right], axis=0)
        for s in range(n // 2 - 1, 0, -1):
            to_right = (part(s) + from_left).astype(dtype)
            to_left = (part(n - s) + from_right).astype(dtype)
            from_left = self.go_right(to_right).astype(F32)
            from_right = self.go_left(to_left).astype(F32)
        return part(0) + from_left + from_right

class Home:
    def __init__(self, ring, far):
        half = far.shape[0] // 2
        self.ring, self.near, self.half = ring, ring.size // 2, half
        self.arrived = ring.go_right(far[:half]), ring.go_left(far[half:])

    def hop(self, to_left, to_right):
        left, right = self.arrived
        if self.near == self.ring.size // 2:
            to_right = jnp.concatenate([to_right[: self.half] + left, to_right[self.half :]], axis=0)
            to_left = jnp.concatenate([to_left[: self.half], to_left[self.half :] + right], axis=0)
        else:
            to_right, to_left = to_right + left, to_left + right
        self.near -= 1
        self.arrived = self.ring.go_right(to_right), self.ring.go_left(to_left)


class Line:
    def __init__(self):
        self.last = ()

    def mark(self, *arrays):
        self.last = arrays

    def tie(self, v):
        return after(v, *self.last) if self.last else v

    def zero(self):
        return zero_of(*self.last).astype(jnp.int32).reshape(1)


class Gather:
    def __init__(self, ring, v):
        self.ring, self.count = ring, 0
        self.got = [v] + [None] * (ring.size - 1)
        self.latest = (v, v)

    def hop(self):
        n, (right, left) = self.ring.size, self.latest
        self.count += 1
        s = self.count
        if s < n // 2:
            self.latest = self.ring.go_right(right), self.ring.go_left(left)
            self.got[s], self.got[n - s] = self.latest
        elif s == n // 2:
            half = right.shape[0] // 2
            self.latest = self.ring.go_right(right[:half]), self.ring.go_left(left[half:])
            self.got[s] = jnp.concatenate(self.latest, axis=0)


def _scores(q, k, row0, scale):
    raw = dot(q, k, ((1,), (1,))) * scale
    rows = lax.broadcasted_iota(jnp.int32, raw.shape, 0) + row0
    cols = lax.broadcasted_iota(jnp.int32, raw.shape, 1)
    return jnp.where(cols <= rows, raw, -1e30)


def _turn(v, cosine, sine):
    return v * cosine + pltpu.roll(v, HEAD_DIM // 2, 1) * sine


def _attend_kernel(place, qp, kp, vp, rq, rk, cosine, sine, gq, gk, o_ref, q_s, k_s, v_s, lse_ref, o_s, *, half, blocks, tile, scale):
    for b in range(blocks):
        at, to = pl.ds(pl.multiple_of(place[b] * half, half), half), slice(b * half, (b + 1) * half)
        c, s = cosine[at, :], sine[at, :]
        q_s[to, :] = _turn(qp[at, :] * rq[at, :] * gq[...], c, s).astype(BF)
        k_s[to, :] = _turn(kp[at, :] * rk[at, :] * gk[...], c, s).astype(BF)
        v_s[to, :] = vp[at, :].astype(BF)
    for i in range(half * blocks // tile):
        width = (i + 1) * tile
        s = _scores(q_s[i * tile : width, :], k_s[:width, :], i * tile, scale)
        top = jnp.max(s, axis=-1, keepdims=True)
        total = top + jnp.log(jnp.sum(jnp.exp(s - top), axis=-1, keepdims=True))
        p = jnp.exp(s - total).astype(BF)
        o_s[i * tile : width, :] = dot(p, v_s[:width, :], ((1,), (0,))).astype(BF)
        lse_ref[0, i * tile : width, :] = total
    for b in range(blocks):
        at = pl.multiple_of(place[b] * half, half)
        o_ref[pl.ds(at, half), :] = o_s[b * half : (b + 1) * half, :]


def _attend_back_kernel(place, q_s, k_s, v_s, d_ref, lse_ref, qp, kp, rq, rk, cosine, sine, gq, gk, wq_ref, wk_ref, dv_ref, in_ref, gain_ref,
                        d_s, dq_s, dk_s, dv_s, *, half, blocks, tile, scale):
    for b in range(blocks):
        at = pl.ds(pl.multiple_of(place[b] * half, half), half)
        d_s[b * half : (b + 1) * half, :] = d_ref[at, :]
    count = half * blocks // tile
    for i in reversed(range(count)):
        width = (i + 1) * tile
        here = slice(i * tile, width)
        q, d, k, v = q_s[here, :], d_s[here, :], k_s[:width, :], v_s[:width, :]
        p = jnp.exp(_scores(q, k, i * tile, scale) - lse_ref[0, here, :])
        dp = dot(d, v, ((1,), (1,)))
        row = jnp.sum(p * dp, axis=-1, keepdims=True)
        ds = (p * (dp - row)).astype(BF)
        dq_s[here, :] = dot(ds, k, ((1,), (0,)))
        dk = dot(ds, q, ((0,), (0,)))
        dv = dot(p.astype(BF), d, ((0,), (0,)))
        if i == count - 1:
            dk_s[:width, :] = dk
            dv_s[:width, :] = dv
        else:
            dk_s[:width, :] += dk
            dv_s[:width, :] += dv

    @pl.when(pl.program_id(0) == 0)
    def _():
        in_ref[...] = jnp.zeros_like(in_ref)

    sums = [jnp.zeros((1, HEAD_DIM), F32)] * 2
    lane = lax.broadcasted_iota(jnp.int32, (1, in_ref.shape[1]), 1)
    for b in range(blocks):
        at, here = pl.ds(pl.multiple_of(place[b] * half, half), half), slice(b * half, (b + 1) * half)
        c, s = cosine[at, :], sine[at, :]
        for n, (grad, pre, r, gain, out) in enumerate(((dq_s, qp, rq, gq, wq_ref), (dk_s, kp, rk, gk, wk_ref))):
            t = _turn(grad[here, :] * scale, c, -s)
            value = pre[at, :]
            w = t * gain[...]
            out[at, :] = w
            in_ref[at, :] += jnp.where(lane == n, jnp.sum(value * w, axis=-1, keepdims=True), 0.0)
            sums[n] = sums[n] + jnp.sum(t * value * r[at, :], axis=0, keepdims=True)
        dv_ref[at, :] = dv_s[here, :].astype(BF)
    gain_ref[0:1, :] = sums[0]
    gain_ref[1:2, :] = sums[1]


def _head_specs(rows, heads):
    head = lambda k: pl.BlockSpec((rows, HEAD_DIM), lambda h, place: (0, k * heads + h))
    lse = pl.BlockSpec((1, rows, 1), lambda h, place: (h, 0, 0))
    col = pl.BlockSpec((rows, 1), lambda h, place: (0, 0))
    table = pl.BlockSpec((rows, HEAD_DIM), lambda h, place: (0, 0))
    gain = pl.BlockSpec((1, HEAD_DIM), lambda h, place: (0, h))
    return head, lse, col, table, gain


def _sizes(rows, half):
    return dict(half=half, blocks=rows // half, tile=min(384, rows), scale=HEAD_DIM**-0.5)


def attend(place, qkv, rq, rk, cosine, sine, gq, gk, half):
    rows, width = qkv.shape[0], qkv.shape[1] // 3
    heads = width // HEAD_DIM
    head, lse, col, table, gain = _head_specs(rows, heads)
    return pl.pallas_call(
        functools.partial(_attend_kernel, **_sizes(rows, half)),
        grid_spec=pltpu.PrefetchScalarGridSpec(
            num_scalar_prefetch=1,
            grid=(heads,),
            in_specs=[head(0), head(1), head(2), col, col, table, table, gain, gain],
            out_specs=[head(0)] * 4 + [lse],
            scratch_shapes=[pltpu.VMEM((rows, HEAD_DIM), BF)],
        ),
        out_shape=[jax.ShapeDtypeStruct((rows, width), BF)] * 4 + [jax.ShapeDtypeStruct((heads, rows, 1), F32)],
        compiler_params=pltpu.CompilerParams(vmem_limit_bytes=VMEM_BYTES),
        cost_estimate=pl.CostEstimate(flops=2 * rows * rows * width * 2, bytes_accessed=20 * rows * width, transcendentals=heads * rows * rows),
        name="attend",
    )(place, qkv, qkv, qkv, rq, rk, cosine, sine, gq, gk)


def attend_back(place, q, k, v, d, lse_in, qkv, rq, rk, cosine, sine, gq, gk, half):
    rows, width = q.shape
    heads = width // HEAD_DIM
    head, lse, col, table, gain = _head_specs(rows, heads)
    return pl.pallas_call(
        functools.partial(_attend_back_kernel, **_sizes(rows, half)),
        grid_spec=pltpu.PrefetchScalarGridSpec(
            num_scalar_prefetch=1,
            grid=(heads,),
            in_specs=[head(0)] * 4 + [lse, head(0), head(1), col, col, table, table, gain, gain],
            out_specs=[head(0)] * 3
            + [pl.BlockSpec((rows, 8), lambda h, place: (0, 0)), pl.BlockSpec((2, HEAD_DIM), lambda h, place: (0, h))],
            scratch_shapes=[pltpu.VMEM((rows, HEAD_DIM), BF)] + [pltpu.VMEM((rows, HEAD_DIM), F32)] * 3,
        ),
        out_shape=[
            jax.ShapeDtypeStruct((rows, width), F32),
            jax.ShapeDtypeStruct((rows, width), F32),
            jax.ShapeDtypeStruct((rows, width), BF),
            jax.ShapeDtypeStruct((rows, 8), F32),
            jax.ShapeDtypeStruct((2, width), F32),
        ],
        compiler_params=pltpu.CompilerParams(vmem_limit_bytes=VMEM_BYTES),
        cost_estimate=pl.CostEstimate(flops=5 * rows * rows * width * 2, bytes_accessed=28 * rows * width, transcendentals=heads * rows * rows),
        name="attend_back",
    )(place, q, k, v, d, lse_in, qkv, qkv, rq, rk, cosine, sine, gq, gk)


def _columns_kernel(place, *refs, pieces, weights, cols):
    for r in range(pieces):
        at = pl.ds(pl.multiple_of(place[r] * cols, cols), cols)
        for w in range(weights):
            refs[pieces + w][:, at] = refs[r][:, w * cols : (w + 1) * cols].astype(F32)


def columns(place, blocks, rows, cols):
    n, tile = len(blocks), min(rows, 64)
    weights = blocks[0].shape[1] // cols
    return pl.pallas_call(
        functools.partial(_columns_kernel, pieces=n, weights=weights, cols=cols),
        grid_spec=pltpu.PrefetchScalarGridSpec(
            num_scalar_prefetch=1,
            grid=(rows // tile,),
            in_specs=[pl.BlockSpec((tile, weights * cols), lambda i, place: (i, 0))] * n,
            out_specs=[pl.BlockSpec((tile, n * cols), lambda i, place: (i, 0))] * weights,
        ),
        out_shape=[jax.ShapeDtypeStruct((rows, n * cols), F32)] * weights,
        compiler_params=pltpu.CompilerParams(vmem_limit_bytes=VMEM_BYTES),
        name="columns",
    )(place, *blocks)


PAD=128

def pick_rows(slot_row, cap):
    return (lax.broadcasted_iota(jnp.int32, (cap, slot_row.shape[1]), 0) == slot_row).astype(BF)

def pick_back(slot_col, cap):
    return (lax.broadcasted_iota(jnp.int32, (slot_col.shape[0], cap), 1) == slot_col).astype(BF)

def _dispatch_kernel(*refs, count, cap):
    slot, rows, w, out_x, out_w = refs[0], refs[1:1+count], refs[1+count], refs[2+count], refs[3+count]
    @pl.when(pl.program_id(1) == 0)
    def _():
        for s in range(count):
            out_x[0, s*cap:(s+1)*cap, :] = dot(pick_rows(slot[s], cap), rows[s][...], ((1,),(0,))).astype(BF)
    out_w[0] = dot(out_x[0], w[0], ((1,),(0,))).astype(BF)

def dispatch(slots, at, rows, w, cap, tile=512):
    n, (J, D, F), T = len(rows), w.shape, rows[0].shape[0]
    M = n * cap
    return pl.pallas_call(
        functools.partial(_dispatch_kernel, count=n, cap=cap),
        grid=(J, F // tile),
        in_specs=[pl.BlockSpec((n, None, 1, T), lambda j, f: (at, j, 0, 0))]
        + [pl.BlockSpec((T, D), lambda j, f: (0, 0), pipeline_mode=pl.Buffered(1))] * n
        + [pl.BlockSpec((1, D, tile), lambda j, f: (j, 0, f))],
        out_specs=[pl.BlockSpec((1, M, D), lambda j, f: (j, 0, 0)), pl.BlockSpec((1, M, tile), lambda j, f: (j, 0, f))],
        out_shape=[jax.ShapeDtypeStruct((J, M, D), BF), jax.ShapeDtypeStruct((J, M, F), BF)],
        compiler_params=pltpu.CompilerParams(vmem_limit_bytes=VMEM_BYTES),
        cost_estimate=pl.CostEstimate(flops=2 * J * M * D * (F + T), bytes_accessed=2 * (J * D * F + n * T * D + J * M * (D + F)), transcendentals=0),
        name="dispatch",
    )(slots, *rows, w)


def _expert_kernel(first, slot, *refs, count, cap, experts):
    rows = refs[:count]
    wg, wu, dw, out_x, out_dg, out_du, out_in, out_dgate, gate = refs[count:]
    D = wg.shape[1]
    f = pl.program_id(1)
    @pl.when(f == 0)
    def _():
        mine = lax.broadcasted_iota(jnp.int32, (1, PAD), 1)
        me = first[0] + pl.program_id(0)
        mask = ((mine == me) | (mine == me + experts)).astype(F32)
        for s in range(count):
            at = slice(s*cap,(s+1)*cap)
            got = dot(pick_rows(slot[s], cap), rows[s][...], ((1,),(0,)))
            out_x[0, at, :] = got[:, :D].astype(BF)
            gate[at, :] = jnp.sum(got[:, D:]*mask, axis=-1, keepdims=True)
        out_dgate[...] = jnp.zeros_like(out_dgate)
    x = out_x[0]
    g = dot(x, wg[0], ((1,),(0,)))
    u = dot(x, wu[0], ((1,),(0,)))
    sig = 1.0/(1.0+jnp.exp(-g))
    act = g*sig
    inner = act*u
    d = dw[0].astype(F32)
    out_dgate[0] += jnp.sum(inner*d, axis=-1, keepdims=True)
    scaled = gate[...]
    d = d*scaled
    out_in[0] = (inner*scaled).astype(BF)
    out_du[0] = (d*act).astype(BF)
    out_dg[0] = (d*u*(sig + act*(1.0-sig))).astype(BF)

def expert(first, slots, at, rows, w_gu, dw, cap, experts, tile=512):
    n=len(rows); J, D2, F = w_gu.shape; D=D2//2; T=rows[0].shape[0]; M=n*cap
    return pl.pallas_call(
        functools.partial(_expert_kernel, count=n, cap=cap, experts=experts),
        grid=(J, F//tile),
        in_specs=[pl.BlockSpec(memory_space=pltpu.SMEM), pl.BlockSpec((n, None, 1, T), lambda j,f:(at,j,0,0))]
          +[pl.BlockSpec((T,D+PAD), lambda j,f:(0,0), pipeline_mode=pl.Buffered(1))]*n
          +[pl.BlockSpec((1,D,tile), lambda j,f:(j,0,f)), pl.BlockSpec((1,D,tile), lambda j,f:(j,1,f)), pl.BlockSpec((1,M,tile), lambda j,f:(j,0,f))],
        out_specs=[pl.BlockSpec((1,M,D), lambda j,f:(j,0,0))]+[pl.BlockSpec((1,M,tile), lambda j,f:(j,0,f))]*3+[pl.BlockSpec((1,M,1), lambda j,f:(j,0,0))],
        out_shape=[jax.ShapeDtypeStruct((J,M,D),BF)]+[jax.ShapeDtypeStruct((J,M,F),BF)]*3+[jax.ShapeDtypeStruct((J,M,1),F32)],
        scratch_shapes=[pltpu.VMEM((M,1),F32)],
        compiler_params=pltpu.CompilerParams(vmem_limit_bytes=VMEM_BYTES),
        cost_estimate=pl.CostEstimate(flops=2*J*M*D*(2*F+T), bytes_accessed=2*(J*D2*F+n*T*D+J*M*(D+4*F)), transcendentals=J*M*F),
        name="expert",
    )(first, slots, *rows, w_gu, w_gu, dw)

def _plus(part, which, more, cols):
    if which is None:
        return part
    more = more[:, cols].astype(F32)
    half = part.shape[0] // 2
    if which == "top":
        return jnp.concatenate([part[:half] + more, part[half:]], axis=0)
    if which == "low":
        return jnp.concatenate([part[:half], part[half:] + more], axis=0)
    return part + more

def _combine_kernel(*refs, terms, count, cap, tile, extra, adds, experts):
    it = iter(refs)
    first = next(it) if extra else None
    slot = next(it)
    factors = [(next(it), next(it)) for _ in range(terms)]
    dgate = next(it) if extra else None
    adds_in = [next(it) if a is not None else None for a in adds]
    outs = [next(it) for _ in range(count)]
    acc = next(it)
    n, j, last = pl.program_id(0), pl.program_id(1), pl.num_programs(1) - 1
    total = None
    for a, w in factors:
        part = dot(a[j], w[0], ((1,),(1,)))
        total = part if total is None else total + part
    total = total.astype(BF)
    cols = pl.ds(pl.multiple_of(n*tile, tile), tile)
    for s in range(count):
        back = pick_back(slot[s, j], cap)
        part = dot(back, total[s*cap:(s+1)*cap], ((1,),(0,)))
        @pl.when(j == 0)
        def _(): acc[s] = _plus(part, adds[s], adds_in[s], cols)
        @pl.when((j > 0) & (j < last))
        def _(): acc[s] += part
        @pl.when(j == last)
        def _(): outs[s][:, cols] = (acc[s] + part).astype(outs[s].dtype)
    if extra:
        D = outs[0].shape[1] - PAD
        @pl.when(n == 0)
        def _():
            lane = lax.broadcasted_iota(jnp.int32, (1, PAD), 1)
            me = first[0] + j
            for s in range(count):
                v = dgate[j, s*cap:(s+1)*cap, :]
                hi = v.astype(BF).astype(F32)
                spread = jnp.where(lane == me, hi, 0.0) + jnp.where(lane == me + experts, v - hi, 0.0)
                part = dot(pick_back(slot[s, j], cap), spread.astype(BF), ((1,),(0,)))
                @pl.when(j == 0)
                def _(): outs[s][:, D:] = _plus(part, adds[s], adds_in[s], slice(D, D + PAD)).astype(outs[s].dtype)
                @pl.when(j > 0)
                def _(): outs[s][:, D:] = (outs[s][:, D:].astype(F32) + part).astype(outs[s].dtype)

def combine(slots, at, factors, cap, adds, first=None, dgate=None, experts=0, tile=1024, out_dtype=BF):
    n = len(adds)
    _, J, T, _ = slots.shape
    M, F = factors[0][0].shape[1:]
    D = factors[-1][1].shape[1] // (factors[-1][2] + 1)
    extra = dgate is not None
    width = D + (PAD if extra else 0)
    steps = D // tile
    one = pl.Buffered(1)
    ops, specs = [], []
    if extra:
        ops.append(first)
        specs.append(pl.BlockSpec(memory_space=pltpu.SMEM))
    ops.append(slots)
    specs.append(pl.BlockSpec((n, J, T, 1), lambda i, j: (at, 0, 0, 0), pipeline_mode=one))
    for a, w, block in factors:
        ops += [a, w]
        specs += [
            pl.BlockSpec((J, M, F), lambda i, j: (0, 0, 0), pipeline_mode=one),
            pl.BlockSpec((1, tile, F), lambda i, j, block=block: (j, block * steps + i, 0)),
        ]
    if extra:
        ops.append(dgate)
        specs.append(pl.BlockSpec((J, M, 1), lambda i, j: (0, 0, 0), pipeline_mode=one))
    for a in adds:
        if a is not None:
            ops.append(a[1])
            specs.append(pl.BlockSpec(a[1].shape, lambda i, j: (0, 0), pipeline_mode=one))
    return pl.pallas_call(
        functools.partial(_combine_kernel, terms=len(factors), count=n, cap=cap, tile=tile, extra=extra, adds=[a and a[0] for a in adds], experts=experts),
        grid=(steps, J),
        in_specs=specs,
        out_specs=[pl.BlockSpec((T, width), lambda i, j: (0, 0))] * n,
        out_shape=[jax.ShapeDtypeStruct((T, width), out_dtype)] * n,
        scratch_shapes=[pltpu.VMEM((n, T, tile), F32)],
        compiler_params=pltpu.CompilerParams(vmem_limit_bytes=VMEM_BYTES),
        cost_estimate=pl.CostEstimate(flops=2 * J * M * D * (len(factors) * F + T), bytes_accessed=2 * len(factors) * J * F * (D + M) + 4 * n * T * D, transcendentals=0),
        name="combine",
    )(*ops)


def _wgrad_kernel(_, *refs, count, pieces):
    xs, gs, outs = refs[:count], refs[count : 2 * count], refs[2 * count :]
    total = None
    for x, g in zip(xs, gs):
        part = dot(x[0], g[0], ((0,), (0,)))
        total = part if total is None else total + part
    for p in range(pieces):

        @pl.when(pl.program_id(2) == p)
        def _(p=p):
            outs[p][0] = total.astype(BF)


def wgrad(order, xs, gs, pieces, tile=2048):
    J, _, D = xs[0].shape
    F = gs[0].shape[2]
    p, n, rows = F // pieces, len(xs), sum(g.shape[1] for g in gs)
    tile = min(tile, D)
    return pl.pallas_call(
        functools.partial(_wgrad_kernel, count=n, pieces=pieces),
        grid=(J, D // tile, pieces),
        in_specs=[pl.BlockSpec(memory_space=pltpu.SMEM)]
        + [pl.BlockSpec((1, x.shape[1], tile), lambda j, i, c: (j, 0, i)) for x in xs]
        + [pl.BlockSpec((1, g.shape[1], p), lambda j, i, c: (j, 0, c)) for g in gs],
        out_specs=[pl.BlockSpec((1, tile, p), lambda j, i, c: (j, i, 0))] * pieces,
        out_shape=[jax.ShapeDtypeStruct((J, D, p), BF)] * pieces,
        compiler_params=pltpu.CompilerParams(vmem_limit_bytes=VMEM_BYTES),
        cost_estimate=pl.CostEstimate(flops=2 * J * rows * D * F, bytes_accessed=2 * J * (rows * (D + F) + D * F), transcendentals=0),
        name="wgrad",
    )(order, *xs, *gs)


def inv_rms(matrix):
    return lax.rsqrt(jnp.mean(matrix * matrix, axis=-1, keepdims=True) + epsilon)


def norm_back(value, gain, grad):
    r = inv_rms(value)
    weighted = gain * grad
    inside = jnp.mean(value * weighted, axis=-1, keepdims=True)
    return r * weighted - value * (r * r * r * inside), jnp.sum(grad * value * r, axis=0)


def angle_tables(positions):
    half_width = HEAD_DIM // 2
    inverse = rope_theta ** (-(jnp.arange(half_width, dtype=F32) * 2.0) / HEAD_DIM)
    angles = positions.astype(F32)[:, None] * inverse[None, :]
    angles = jnp.concatenate([angles, angles], axis=-1)
    sign = jnp.where(jnp.arange(HEAD_DIM) < half_width, -1.0, 1.0)
    return jnp.cos(angles), jnp.sin(angles) * sign


def per_device(
    exp_walk,
    layer_input,
    block_ids,
    routes,
    w_query,
    w_key,
    w_value,
    w_output,
    w_router,
    norm_gains,
    w_gate_up,
    w_down,
    d_out,
):
    C, E = lax.axis_size("ctx"), lax.axis_size("exp")
    c, e = lax.axis_index("ctx"), lax.axis_index("exp")
    Y = C // CORES
    ring = Ring("exp", [exp_walk])
    ctx_ring = Ring("ctx", [[y * CORES + k for y in range(Y)] for k in range(CORES)])
    sibling = [(i, i ^ 1) for i in range(C)]

    def swap(v):
        return lax.ppermute(v, "ctx", sibling)

    def ctx_gather(v):
        got = []
        for block in ctx_ring.gather(v):
            got += [block, swap(block)]
        return got

    def chip_sums(part):
        return [part(dy * CORES).astype(F32) + swap(part(dy * CORES + 1).astype(BF)).astype(F32) for dy in range(Y)]

    def y_sum(mine):
        return ctx_ring.scatter(lambda s: mine[(Y - s) % Y])

    def ctx_sum(rows):
        n = rows.shape[0]
        blocks = jnp.transpose(rows.reshape(n, C, -1), (1, 0, 2))
        whole = jnp.zeros_like(blocks)
        for r in range(C):
            whole = lax.dynamic_update_slice(whole, blocks[r : r + 1], (other_u[r], zero, zero))
        whole = lax.psum(whole, "ctx")
        return jnp.concatenate([lax.dynamic_index_in_dim(whole, other_u[r], 0, False) for r in range(C)], axis=1)

    zero = jnp.uint32(0)
    where = {d: i for i, d in enumerate(exp_walk)}
    left_table = [[exp_walk[(where[i] - s) % E] for s in range(E)] for i in range(E)]
    left_now = lax.dynamic_index_in_dim(jnp.array(left_table, jnp.uint32), e.astype(jnp.uint32), 0, False)
    left_of = [left_now[s] for s in range(E)]

    def put_rows(blocks):
        full = jnp.zeros((E, *blocks[0].shape), BF)
        for s in range(E):
            full = lax.dynamic_update_slice(full, blocks[s][None], (left_of[s], zero, zero))
        return full
    ctx_table = [
        [(i // CORES - r // CORES) % Y * CORES + (i % CORES ^ r % CORES) for r in range(C)] for i in range(C)
    ]
    others = lax.dynamic_index_in_dim(jnp.array(ctx_table, jnp.int32), c.astype(jnp.uint32), 0, False)
    other_u = [others[r].astype(jnp.uint32) for r in range(C)]

    T, D = layer_input.shape[1:]
    rows_e = w_query.shape[0]
    cols_c = D // C
    S = T * C
    half = T // 2
    c_col = (c * cols_c).astype(jnp.uint32)
    NE = w_router.shape[1]
    K = routes.shape[2]
    J = w_gate_up.shape[0]
    cap = (5 * T * K + 4 * NE - 1) // (4 * NE)
    room = -(-cap // 16) * 16
    x = layer_input[0]
    grad_out = d_out[0]

    x_blocks = ctx_gather(x)
    x_all = jnp.concatenate(x_blocks, axis=0)

    small = jnp.concatenate([w_router.reshape(-1), norm_gains.reshape(-1), routes.astype(BF).reshape(-1)])
    small_len = small.shape[0]
    small = jnp.pad(small, (0, -small_len % 4096)).reshape(-1, 128)
    w_qkv_mine = jnp.concatenate(
        [lax.dynamic_slice_in_dim(w, c_col, cols_c, axis=1) for w in (w_query, w_key, w_value)], axis=1
    )
    qkv_walk, small_walk = Gather(ring, w_qkv_mine), Gather(ring, small)
    for _ in range(E // 2):
        small_walk.hop()
        qkv_walk.hop()
        if qkv_walk.count == 2:
            qkv_walk.latest = [v + zero_of(x_blocks[-CORES]).astype(BF) for v in qkv_walk.latest]
        small_walk.latest = [after(v, *qkv_walk.latest) for v in small_walk.latest]
    order = [E // 2, 0] + [i for s in range(1, E // 2) for i in (s, E - s)]
    small_all = jnp.stack([small_walk.got[i] for i in order])
    by_owner = put_rows(small_walk.got)
    cut = rows_e * NE // 128, rows_e * (NE + norm_gains.shape[1]) // 128, small_len // 128
    router_full = by_owner[:, : cut[0]].reshape(D, NE)
    gains = by_owner[:, cut[0] : cut[1]].reshape(D, -1).astype(F32).T
    routes_all = small_all[:, cut[1] : cut[2]].reshape(E, T * K)

    def my_columns(w):
        return lax.dynamic_slice_in_dim(w, c_col, cols_c, axis=1)

    qkv_blocks = qkv_walk.got
    w_qkv = put_rows(qkv_blocks).reshape(D, 3 * cols_c)
    qkv_there = qkv_blocks[E // 2]
    w_out_cols = lax.all_gather(my_columns(w_output), "exp", axis=0, tiled=True)
    w_out_rows = lax.all_to_all(w_out_cols.reshape(C, cols_c, cols_c), "ctx", split_axis=0, concat_axis=0, tiled=True)
    w_out_rows = jnp.transpose(w_out_rows, (1, 0, 2)).reshape(cols_c, D)

    d_walk = Gather(ring, after(grad_out, qkv_there))
    d_walk.hop()
    dn_blocks = ctx_gather(w_down)
    w_dn = jnp.concatenate(dn_blocks, axis=2)

    def hold(v, *others):
        return v + zero_of(*others).astype(v.dtype)

    gu_first = ctx_gather(hold(w_gate_up[: J // 2], dn_blocks[-CORES]))

    blocks_rel = jnp.stack([lax.dynamic_slice_in_dim(block_ids[0], other_u[r] * 2, 2) for r in range(C)]).reshape(-1)
    positions = (blocks_rel[:, None] * half + jnp.arange(half, dtype=jnp.int32)[None, :]).reshape(-1)
    count = jnp.arange(2 * C, dtype=jnp.int32)
    place = jnp.sum(jnp.where(blocks_rel[None, :] == count[:, None], count[None, :], 0), axis=1)
    cosine, sine = angle_tables(positions)
    gain_q = lax.dynamic_slice_in_dim(gains[1:2], c_col, cols_c, axis=1)
    gain_k = lax.dynamic_slice_in_dim(gains[2:3], c_col, cols_c, axis=1)

    groups = [([0], 1)] + [([s, E - s], s) for s in range(1, E // 2)] + [([E // 2], 0)]
    first = (e * J).astype(jnp.int32).reshape(1)
    mine = first[0] + jnp.arange(J, dtype=jnp.int32)
    pairs = (routes_all[:, None, :] == mine[None, :, None].astype(BF)).astype(BF).reshape(E * J, T * K)
    token = jnp.arange(T * K)[:, None] // K
    chosen = dot(pairs, (token == jnp.arange(T)[None, :]).astype(BF), ((1,), (0,)))
    rank = dot(pairs, (token < jnp.arange(T)[None, :]).astype(BF), ((1,), (0,)))
    slot = jnp.where((chosen > 0.5) & (rank < cap), rank, -1.0).astype(jnp.int32).reshape(E, J, T)
    slot_row, slot_col = slot[:, :, None, :], slot[:, :, :, None]

    line, d_slots = Line(), {}

    def fetch(g):
        members, at = groups[g]
        d_slots[g] = dispatch(line.tie(slot_row), at, [d_walk.got[i] for i in members], w_dn, room)
        line.mark(d_slots[g][1])

    fetch(0)
    x_all32 = x_all.astype(F32)
    n1 = (x_all32 * inv_rms(x_all32) * gains[0]).astype(BF)
    qkv = dot(n1, w_qkv, ((1,), (0,)))
    qp, kp = qkv[:, :cols_c], qkv[:, cols_c : 2 * cols_c]
    squares = hold(jnp.stack([jnp.sum(qp * qp, axis=1), jnp.sum(kp * kp, axis=1)]), gu_first[-CORES], d_slots[0][1])
    scales = lax.rsqrt(ctx_sum(squares) / D + epsilon)
    r_q, r_k = scales[0][:, None], scales[1][:, None]
    d_walk.latest = [hold(v, scales) for v in d_walk.latest]
    d_walk.hop()
    gu_last = ctx_gather(hold(w_gate_up[J // 2 :], scales))
    w_gu = jnp.concatenate([jnp.concatenate(b, axis=2) for b in (gu_first, gu_last)], axis=0)
    attn, q, k, v, lse = attend(place, qkv, r_q, r_k, cosine, sine, gain_q, gain_k, half)
    branch_part = dot(attn, w_out_rows, ((1,), (0,))).astype(BF)
    chips = chip_sums(lambda r: branch_part[r * T : (r + 1) * T])
    branch = y_sum([hold(v, gu_last[-CORES]) for v in chips])
    d_walk.latest = [hold(v, branch_part) for v in d_walk.latest]
    while d_walk.count < E // 2 - 1:
        d_walk.hop()
    line.mark(branch_part)
    fetch(1)
    branch = hold(branch, w_gu, d_slots[1][1])
    hidden = x.astype(F32) + branch
    n2 = (hidden * inv_rms(hidden) * gains[3]).astype(BF)
    router_own = jax.nn.softmax(dot(n2, router_full, ((1,), (0,))), axis=-1)
    router_high = router_own.astype(BF)
    router_low = (router_own - router_high.astype(F32)).astype(BF)
    n2_wide = jnp.concatenate([n2, router_high, router_low, jnp.zeros((T, PAD - 2 * NE), BF)], axis=1)

    line, n2_walk, done = Line(), Gather(ring, n2_wide), {}

    def work(g):
        members, at = groups[g]
        done[g] = expert(first, line.tie(slot_row), at, [n2_walk.got[i] for i in members], w_gu, d_slots[g][1], room, NE)
        line.mark(done[g][1])

    def back(g):
        members, at = groups[g]
        _, dg, du, _, dgate = done[g]
        kind = F32 if members == [0] else BF
        got = combine(line.tie(slot_col), at, [(dg, w_gu, 0), (du, w_gu, 1)], room, [None] * len(members), first, dgate, NE, out_dtype=kind)
        line.mark(got[0])
        return got

    def mix(g):
        members, at = groups[g]
        kind = F32 if members == [0] else BF
        got = combine(line.tie(slot_col), at, [(done[g][3], w_dn, 0)], room, [None] * len(members), out_dtype=kind)
        line.mark(got[0])
        return got

    def grads(left, right):
        parts = wgrad(line.zero(), left, right, C)
        line.mark(parts[0])
        return chip_sums(lambda r: parts[r])

    far = E // 2
    n2_walk.hop()
    d_walk.latest = [hold(v, n2_wide) for v in d_walk.latest]
    d_walk.hop()
    line.mark(n2_wide)
    work(0)
    fetch(2)
    for g in range(1, far + 1):
        line.mark(*n2_walk.latest, line.last[0])
        if g < far:
            n2_walk.hop()
        work(g)
        if g + 1 < far:
            fetch(g + 2)
    home = Home(ring, back(far)[0])
    for g in range(far - 1, 0, -1):
        terms = back(g)
        line.mark(*home.arrived, line.last[0])
        home.hop(*terms)
    [own] = back(0)
    chips_g = grads([done[i][0] for i in done], [done[i][1] for i in done])
    [mix_far] = mix(far)
    line.mark(*home.arrived, line.last[0])
    rows_back = own + home.arrived[0].astype(F32) + home.arrived[1].astype(F32)
    mixed = Home(ring, after(mix_far, *home.arrived))
    drouter = rows_back[:, D : D + NE] + rows_back[:, D + NE : D + 2 * NE]
    dlogits = (router_own * (drouter - jnp.sum(drouter * router_own, axis=-1, keepdims=True))).astype(BF)
    dn2 = rows_back[:, :D] + dot(dlogits, router_full, ((1,), (1,)))
    hidden_part, d_gain3 = norm_back(hidden, gains[3], dn2)
    dhidden = grad_out.astype(F32) + hidden_part
    dhidden_low = dhidden.astype(BF)
    dhidden_blocks = ctx_gather(dhidden_low)
    dhidden_all = jnp.concatenate(dhidden_blocks, axis=0)
    line.mark(dhidden_low)
    terms = {}
    for g in range(far - 1, -1, -1):
        terms[g] = mix(g)
        if g == far - 1:
            line.mark(*mixed.arrived, line.last[0])
            mixed.hop(*terms[g])
            line.mark(*terms[g])
            chips_u = grads([done[i][0] for i in done], [done[i][2] for i in done])
    sum_g = y_sum([hold(v, dhidden_blocks[-CORES]) for v in chips_g])

    def pump():
        if mixed.near > 1:
            line.mark(*mixed.arrived, *line.last)
            mixed.hop(*terms[mixed.near - 1])

    dattn = dot(after(dhidden_all, *line.last), w_out_rows, ((1,), (1,))).astype(BF)
    g_out = dot(attn, dhidden_all, ((0,), (0,))).astype(BF)
    line.mark(g_out, dattn)
    pump()
    wq, wk, dv, inside, d_gain_qk = attend_back(line.tie(place), q, k, v, dattn, lse, qkv, r_q, r_k, cosine, sine, gain_q, gain_k, half)
    line.mark(dv)
    pump()
    def next_hop(walk, of):
        if walk.near > 1:
            line.mark(*walk.arrived, *line.last)
            walk.hop(of(walk.near - 1), of(E - walk.near + 1))

    g_out = jnp.transpose(g_out.reshape(cols_c, C, cols_c), (1, 0, 2))
    g_out = lax.all_to_all(g_out, "ctx", split_axis=0, concat_axis=0, tiled=True).reshape(E, rows_e, cols_c)
    g_router = dot(dlogits, n2, ((0,), (0,)))
    spread = lax.dynamic_update_slice(jnp.zeros((2, D), F32), d_gain_qk, (zero, c_col))
    g_small = jnp.concatenate([g_router, spread, d_gain3[None]], axis=0)
    count = g_small.shape[0]
    g_small = jnp.transpose(g_small.reshape(count, E, rows_e), (1, 0, 2)).reshape(E, -1)
    unit = 3 * 16
    small_rows = -(-(rows_e * cols_c + count * rows_e) // (cols_c * unit)) * unit - rows_e
    g_small = jnp.pad(g_small, ((0, 0), (0, small_rows * cols_c - count * rows_e))).reshape(E, small_rows, cols_c)
    more = jnp.concatenate([g_out, g_small.astype(BF)], axis=1).reshape(E, -1, 3 * cols_c)
    more = lax.optimization_barrier(more)

    inside = ctx_sum(hold(line.tie(inside)[:, :2].T, sum_g, more)) / D
    dqp = r_q * wq - qp * (r_q * r_q * r_q * inside[0][:, None])
    dkp = r_k * wk - kp * (r_k * r_k * r_k * inside[1][:, None])
    dqkv = jnp.concatenate([dqp.astype(BF), dkp.astype(BF), dv], axis=1)
    g_qkv = dot(n1, dqkv, ((0,), (0,))).astype(BF).reshape(E, rows_e, 3 * cols_c)

    def of_qkv(s):
        return jnp.concatenate([lax.dynamic_index_in_dim(a, left_of[s], 0, False) for a in (g_qkv, more)], axis=0)

    qkv_home = Home(ring, of_qkv(far))
    sum_u = y_sum([hold(v, inside) for v in chips_u])
    line.mark(g_qkv)
    dn1_part = dot(line.tie(dqkv), w_qkv, ((1,), (1,))).astype(BF)
    line.mark(dn1_part)
    next_hop(qkv_home, lambda s: hold(of_qkv(s), sum_u))
    chips_n1 = chip_sums(lambda r: dn1_part[r * T : (r + 1) * T])
    dn1 = y_sum(chips_n1)
    line.mark(dn1_part)
    chips_d = grads([d_slots[i][0] for i in done], [done[i][3] for i in done])
    next_hop(qkv_home, of_qkv)
    sum_d = y_sum(chips_d)

    def arrived_sum(walk, own):
        return own.astype(F32) + walk.arrived[0].astype(F32) + walk.arrived[1].astype(F32)

    while qkv_home.near > 1:
        next_hop(qkv_home, lambda s: hold(of_qkv(s), sum_d))
    x32 = x.astype(F32)
    token_part, _ = norm_back(x32, gains[0], dn1)
    d_x = (dhidden + token_part)[None]
    g_gate_up = jnp.concatenate([sum_g, sum_u], axis=1)
    g_down = sum_d
    while mixed.near > 1:
        pump()
    output = (hidden + terms[0][0] + mixed.arrived[0].astype(F32) + mixed.arrived[1].astype(F32)).astype(BF)[None]

    dense_mine = arrived_sum(qkv_home, of_qkv(0))
    g_qkv_mine = dense_mine[:rows_e]
    own_gain = norm_gains[:, 0].astype(F32)
    d_gain0 = jnp.sum(w_qkv_mine.astype(F32) * g_qkv_mine, axis=1) / own_gain
    gain_rows = -(-rows_e // (3 * cols_c * 16)) * 16
    d_gain0 = jnp.pad(d_gain0, (0, gain_rows * 3 * cols_c - rows_e)).reshape(gain_rows, 3 * cols_c)
    pieces = ctx_gather(jnp.concatenate([dense_mine, d_gain0], axis=0).astype(BF))
    g_query, g_key, g_value = columns(others, pieces, rows_e, cols_c)
    last = dense_mine.shape[0]
    out_pieces = [p[rows_e:last].reshape(-1, cols_c) for p in pieces]
    [g_output] = columns(others, out_pieces, rows_e, cols_c)
    g_small = sum(p[rows_e:].astype(F32) for p in out_pieces).reshape(-1)[: count * rows_e].reshape(count, rows_e)
    d_gain0 = sum(p[last:].astype(F32) for p in pieces).reshape(-1)[:rows_e]
    g_gains = jnp.concatenate([d_gain0[None], g_small[NE:]], axis=0).T
    return (output, d_x, g_query, g_key, g_value, g_output, g_small[:NE].T, g_gains, g_gate_up, g_down)


def solution(mesh):
    exp_walk = ring_order(mesh.shape["exp"])
    tokens = P("exp", "ctx", None)
    rows = P("exp", None)
    hidden_units = P("exp", None, "ctx")
    in_specs = (tokens, rows, tokens) + (rows,) * 6 + (hidden_units, hidden_units, tokens)
    out_specs = (tokens, tokens) + (rows,) * 6 + (hidden_units, hidden_units)
    return jax.shard_map(
        functools.partial(per_device, exp_walk),
        mesh=mesh,
        in_specs=in_specs,
        out_specs=out_specs,
        check_vma=False,
    )
```

```python
import functools

import jax
import jax.numpy as jnp
from jax import lax
from jax.experimental import pallas as pl
from jax.experimental.pallas import tpu as pltpu
from jax.sharding import PartitionSpec as P

HEAD_DIM = 128
CORES = 2
ROWS_Z = 4
VMEM_BYTES = 56 << 20

epsilon = 1e-05
rope_theta = 10000.0
BF = jnp.bfloat16
F32 = jnp.float32


def dot(a, b, dims):
    return lax.dot_general(a, b, (dims, ((), ())), preferred_element_type=F32)


def after(v, *others):
    return lax.optimization_barrier((v, *others))[0]


def zero_of(*arrays):
    return sum(a[(0,) * a.ndim].astype(F32) for a in arrays) * 0.0


def ring_order(count):
    rows = ROWS_Z if count % ROWS_Z == 0 else 1
    across = count // rows
    walk = [(0, 0)]
    for z in range(rows):
        xs = range(1, across)
        walk += [(z, x) for x in (xs if z % 2 == 0 else reversed(xs))]
    walk += [(z, 0) for z in range(rows - 1, 0, -1)]
    return [z * across + x for z, x in walk]


class Ring:
    def __init__(self, axis, rings):
        self.axis = axis
        self.size = len(rings[0])
        self.right = [
            (r[i], r[(i + 1) % self.size]) for r in rings for i in range(self.size)
        ]
        self.left = [(b, a) for a, b in self.right]

    def go_right(self, v):
        return lax.ppermute(v, self.axis, self.right)

    def go_left(self, v):
        return lax.ppermute(v, self.axis, self.left)

    def gather(self, v):
        if self.size == 2:
            return [v, self.go_right(v)]
        walk = Gather(self, v)
        for _ in range(self.size // 2):
            walk.hop()
        return walk.got

    def scatter(self, part, dtype=BF):
        n = self.size
        far = part(n // 2).astype(dtype)
        if n == 2:
            return part(0) + self.go_right(far).astype(F32)
        half = far.shape[0] // 2
        from_left = self.go_right(far[:half]).astype(F32)
        from_right = self.go_left(far[half:]).astype(F32)
        from_left = jnp.concatenate([from_left, jnp.zeros_like(from_left)], axis=0)
        from_right = jnp.concatenate([jnp.zeros_like(from_right), from_right], axis=0)
        for s in range(n // 2 - 1, 0, -1):
            to_right = (part(s) + from_left).astype(dtype)
            to_left = (part(n - s) + from_right).astype(dtype)
            from_left = self.go_right(to_right).astype(F32)
            from_right = self.go_left(to_left).astype(F32)
        return part(0) + from_left + from_right

class Home:
    def __init__(self, ring, far):
        half = far.shape[0] // 2
        self.ring, self.near, self.half = ring, ring.size // 2, half
        self.arrived = ring.go_right(far[:half]), ring.go_left(far[half:])

    def hop(self, to_left, to_right):
        left, right = self.arrived
        if self.near == self.ring.size // 2:
            to_right = jnp.concatenate([to_right[: self.half] + left, to_right[self.half :]], axis=0)
            to_left = jnp.concatenate([to_left[: self.half], to_left[self.half :] + right], axis=0)
        else:
            to_right, to_left = to_right + left, to_left + right
        self.near -= 1
        self.sent = to_right, to_left
        self.arrived = self.ring.go_right(to_right), self.ring.go_left(to_left)


class Line:
    def __init__(self):
        self.last = ()

    def mark(self, *arrays):
        self.last = arrays

    def tie(self, v):
        return after(v, *self.last) if self.last else v

    def zero(self):
        return zero_of(*self.last).astype(jnp.int32).reshape(1)


class Gather:
    def __init__(self, ring, v):
        self.ring, self.count = ring, 0
        self.got = [v] + [None] * (ring.size - 1)
        self.latest = (v, v)

    def hop(self):
        n, (right, left) = self.ring.size, self.latest
        self.count += 1
        s = self.count
        if s < n // 2:
            self.latest = self.ring.go_right(right), self.ring.go_left(left)
            self.got[s], self.got[n - s] = self.latest
        elif s == n // 2:
            half = right.shape[0] // 2
            self.latest = self.ring.go_right(right[:half]), self.ring.go_left(left[half:])
            self.got[s] = jnp.concatenate(self.latest, axis=0)


def _scores(q, k, row0, scale):
    raw = dot(q, k, ((1,), (1,))) * scale
    rows = lax.broadcasted_iota(jnp.int32, raw.shape, 0) + row0
    cols = lax.broadcasted_iota(jnp.int32, raw.shape, 1)
    return jnp.where(cols <= rows, raw, -1e30)


def _turn(v, cosine, sine):
    return v * cosine + pltpu.roll(v, HEAD_DIM // 2, 1) * sine


def _attend_kernel(place, qp, kp, vp, rq, rk, cosine, sine, gq, gk, o_ref, q_s, k_s, v_s, lse_ref, o_s, *, half, blocks, tile, scale):
    for b in range(blocks):
        at, to = pl.ds(pl.multiple_of(place[b] * half, half), half), slice(b * half, (b + 1) * half)
        c, s = cosine[at, :], sine[at, :]
        q_s[to, :] = _turn(qp[at, :] * rq[at, :] * gq[...], c, s).astype(BF)
        k_s[to, :] = _turn(kp[at, :] * rk[at, :] * gk[...], c, s).astype(BF)
        v_s[to, :] = vp[at, :].astype(BF)
    for i in range(half * blocks // tile):
        width = (i + 1) * tile
        s = _scores(q_s[i * tile : width, :], k_s[:width, :], i * tile, scale)
        top = jnp.max(s, axis=-1, keepdims=True)
        total = top + jnp.log(jnp.sum(jnp.exp(s - top), axis=-1, keepdims=True))
        p = jnp.exp(s - total).astype(BF)
        o_s[i * tile : width, :] = dot(p, v_s[:width, :], ((1,), (0,))).astype(BF)
        lse_ref[0, i * tile : width, :] = total
    for b in range(blocks):
        at = pl.multiple_of(place[b] * half, half)
        o_ref[pl.ds(at, half), :] = o_s[b * half : (b + 1) * half, :]


def _attend_back_kernel(place, q_s, k_s, v_s, d_ref, lse_ref, qp, kp, rq, rk, cosine, sine, gq, gk, wq_ref, wk_ref, dv_ref, in_ref, gain_ref,
                        d_s, dq_s, dk_s, dv_s, *, half, blocks, tile, scale):
    for b in range(blocks):
        at = pl.ds(pl.multiple_of(place[b] * half, half), half)
        d_s[b * half : (b + 1) * half, :] = d_ref[at, :]
    count = half * blocks // tile
    for i in reversed(range(count)):
        width = (i + 1) * tile
        here = slice(i * tile, width)
        q, d, k, v = q_s[here, :], d_s[here, :], k_s[:width, :], v_s[:width, :]
        p = jnp.exp(_scores(q, k, i * tile, scale) - lse_ref[0, here, :])
        dp = dot(d, v, ((1,), (1,)))
        row = jnp.sum(p * dp, axis=-1, keepdims=True)
        ds = (p * (dp - row)).astype(BF)
        dq_s[here, :] = dot(ds, k, ((1,), (0,)))
        dk = dot(ds, q, ((0,), (0,)))
        dv = dot(p.astype(BF), d, ((0,), (0,)))
        if i == count - 1:
            dk_s[:width, :] = dk
            dv_s[:width, :] = dv
        else:
            dk_s[:width, :] += dk
            dv_s[:width, :] += dv

    @pl.when(pl.program_id(0) == 0)
    def _():
        in_ref[...] = jnp.zeros_like(in_ref)

    sums = [jnp.zeros((1, HEAD_DIM), F32)] * 2
    lane = lax.broadcasted_iota(jnp.int32, (1, in_ref.shape[1]), 1)
    for b in range(blocks):
        at, here = pl.ds(pl.multiple_of(place[b] * half, half), half), slice(b * half, (b + 1) * half)
        c, s = cosine[at, :], sine[at, :]
        for n, (grad, pre, r, gain, out) in enumerate(((dq_s, qp, rq, gq, wq_ref), (dk_s, kp, rk, gk, wk_ref))):
            t = _turn(grad[here, :] * scale, c, -s)
            value = pre[at, :]
            w = t * gain[...]
            out[at, :] = w
            in_ref[at, :] += jnp.where(lane == n, jnp.sum(value * w, axis=-1, keepdims=True), 0.0)
            sums[n] = sums[n] + jnp.sum(t * value * r[at, :], axis=0, keepdims=True)
        dv_ref[at, :] = dv_s[here, :].astype(BF)
    gain_ref[0:1, :] = sums[0]
    gain_ref[1:2, :] = sums[1]


def _head_specs(rows, heads):
    head = lambda k: pl.BlockSpec((rows, HEAD_DIM), lambda h, place: (0, k * heads + h))
    lse = pl.BlockSpec((1, rows, 1), lambda h, place: (h, 0, 0))
    col = pl.BlockSpec((rows, 1), lambda h, place: (0, 0))
    table = pl.BlockSpec((rows, HEAD_DIM), lambda h, place: (0, 0))
    gain = pl.BlockSpec((1, HEAD_DIM), lambda h, place: (0, h))
    return head, lse, col, table, gain


def _sizes(rows, half):
    return dict(half=half, blocks=rows // half, tile=min(384, rows), scale=HEAD_DIM**-0.5)


def attend(place, qkv, rq, rk, cosine, sine, gq, gk, half):
    rows, width = qkv.shape[0], qkv.shape[1] // 3
    heads = width // HEAD_DIM
    head, lse, col, table, gain = _head_specs(rows, heads)
    return pl.pallas_call(
        functools.partial(_attend_kernel, **_sizes(rows, half)),
        grid_spec=pltpu.PrefetchScalarGridSpec(
            num_scalar_prefetch=1,
            grid=(heads,),
            in_specs=[head(0), head(1), head(2), col, col, table, table, gain, gain],
            out_specs=[head(0)] * 4 + [lse],
            scratch_shapes=[pltpu.VMEM((rows, HEAD_DIM), BF)],
        ),
        out_shape=[jax.ShapeDtypeStruct((rows, width), BF)] * 4 + [jax.ShapeDtypeStruct((heads, rows, 1), F32)],
        compiler_params=pltpu.CompilerParams(vmem_limit_bytes=VMEM_BYTES),
        cost_estimate=pl.CostEstimate(flops=2 * rows * rows * width * 2, bytes_accessed=20 * rows * width, transcendentals=heads * rows * rows),
        name="attend",
    )(place, qkv, qkv, qkv, rq, rk, cosine, sine, gq, gk)


def attend_back(place, q, k, v, d, lse_in, qkv, rq, rk, cosine, sine, gq, gk, half):
    rows, width = q.shape
    heads = width // HEAD_DIM
    head, lse, col, table, gain = _head_specs(rows, heads)
    return pl.pallas_call(
        functools.partial(_attend_back_kernel, **_sizes(rows, half)),
        grid_spec=pltpu.PrefetchScalarGridSpec(
            num_scalar_prefetch=1,
            grid=(heads,),
            in_specs=[head(0)] * 4 + [lse, head(0), head(1), col, col, table, table, gain, gain],
            out_specs=[head(0)] * 3
            + [pl.BlockSpec((rows, 8), lambda h, place: (0, 0)), pl.BlockSpec((2, HEAD_DIM), lambda h, place: (0, h))],
            scratch_shapes=[pltpu.VMEM((rows, HEAD_DIM), BF)] + [pltpu.VMEM((rows, HEAD_DIM), F32)] * 3,
        ),
        out_shape=[
            jax.ShapeDtypeStruct((rows, width), F32),
            jax.ShapeDtypeStruct((rows, width), F32),
            jax.ShapeDtypeStruct((rows, width), BF),
            jax.ShapeDtypeStruct((rows, 8), F32),
            jax.ShapeDtypeStruct((2, width), F32),
        ],
        compiler_params=pltpu.CompilerParams(vmem_limit_bytes=VMEM_BYTES),
        cost_estimate=pl.CostEstimate(flops=5 * rows * rows * width * 2, bytes_accessed=28 * rows * width, transcendentals=heads * rows * rows),
        name="attend_back",
    )(place, q, k, v, d, lse_in, qkv, qkv, rq, rk, cosine, sine, gq, gk)


def _columns_kernel(place, *refs, pieces, weights, cols):
    for r in range(pieces):
        at = pl.ds(pl.multiple_of(place[r] * cols, cols), cols)
        for w in range(weights):
            refs[pieces + w][:, at] = refs[r][:, w * cols : (w + 1) * cols].astype(F32)


def columns(place, blocks, rows, cols):
    n, tile = len(blocks), min(rows, 64)
    weights = blocks[0].shape[1] // cols
    return pl.pallas_call(
        functools.partial(_columns_kernel, pieces=n, weights=weights, cols=cols),
        grid_spec=pltpu.PrefetchScalarGridSpec(
            num_scalar_prefetch=1,
            grid=(rows // tile,),
            in_specs=[pl.BlockSpec((tile, weights * cols), lambda i, place: (i, 0))] * n,
            out_specs=[pl.BlockSpec((tile, n * cols), lambda i, place: (i, 0))] * weights,
        ),
        out_shape=[jax.ShapeDtypeStruct((rows, n * cols), F32)] * weights,
        compiler_params=pltpu.CompilerParams(vmem_limit_bytes=VMEM_BYTES),
        name="columns",
    )(place, *blocks)


PAD=128

def pick_rows(slot_row, cap):
    return (lax.broadcasted_iota(jnp.int32, (cap, slot_row.shape[1]), 0) == slot_row).astype(BF)

def pick_back(slot_col, cap):
    return (lax.broadcasted_iota(jnp.int32, (slot_col.shape[0], cap), 1) == slot_col).astype(BF)

def _dispatch_kernel(*refs, count, cap):
    slot, rows, w, out_x, out_w = refs[0], refs[1:1+count], refs[1+count], refs[2+count], refs[3+count]
    @pl.when(pl.program_id(1) == 0)
    def _():
        for s in range(count):
            out_x[0, s*cap:(s+1)*cap, :] = dot(pick_rows(slot[s], cap), rows[s][...], ((1,),(0,))).astype(BF)
    out_w[0] = dot(out_x[0], w[0], ((1,),(0,))).astype(BF)

def dispatch(slots, at, rows, w, cap, tile=512):
    n, (J, D, F), T = len(rows), w.shape, rows[0].shape[0]
    M = n * cap
    return pl.pallas_call(
        functools.partial(_dispatch_kernel, count=n, cap=cap),
        grid=(J, F // tile),
        in_specs=[pl.BlockSpec((n, None, 1, T), lambda j, f: (at, j, 0, 0))]
        + [pl.BlockSpec((T, D), lambda j, f: (0, 0), pipeline_mode=pl.Buffered(1))] * n
        + [pl.BlockSpec((1, D, tile), lambda j, f: (j, 0, f))],
        out_specs=[pl.BlockSpec((1, M, D), lambda j, f: (j, 0, 0)), pl.BlockSpec((1, M, tile), lambda j, f: (j, 0, f))],
        out_shape=[jax.ShapeDtypeStruct((J, M, D), BF), jax.ShapeDtypeStruct((J, M, F), BF)],
        compiler_params=pltpu.CompilerParams(vmem_limit_bytes=VMEM_BYTES),
        cost_estimate=pl.CostEstimate(flops=2 * J * M * D * (F + T), bytes_accessed=2 * (J * D * F + n * T * D + J * M * (D + F)), transcendentals=0),
        name="dispatch",
    )(slots, *rows, w)


def _expert_kernel(first, slot, *refs, count, cap, experts):
    rows = refs[:count]
    wg, wu, dw, out_x, out_dg, out_du, out_in, out_dgate, gate = refs[count:]
    D = wg.shape[1]
    f = pl.program_id(1)
    @pl.when(f == 0)
    def _():
        mine = lax.broadcasted_iota(jnp.int32, (1, PAD), 1)
        me = first[0] + pl.program_id(0)
        mask = ((mine == me) | (mine == me + experts)).astype(F32)
        for s in range(count):
            at = slice(s*cap,(s+1)*cap)
            got = dot(pick_rows(slot[s], cap), rows[s][...], ((1,),(0,)))
            out_x[0, at, :] = got[:, :D].astype(BF)
            gate[at, :] = jnp.sum(got[:, D:]*mask, axis=-1, keepdims=True)
        out_dgate[...] = jnp.zeros_like(out_dgate)
    x = out_x[0]
    g = dot(x, wg[0], ((1,),(0,)))
    u = dot(x, wu[0], ((1,),(0,)))
    sig = 1.0/(1.0+jnp.exp(-g))
    act = g*sig
    inner = act*u
    d = dw[0].astype(F32)
    out_dgate[0] += jnp.sum(inner*d, axis=-1, keepdims=True)
    scaled = gate[...]
    d = d*scaled
    out_in[0] = (inner*scaled).astype(BF)
    out_du[0] = (d*act).astype(BF)
    out_dg[0] = (d*u*(sig + act*(1.0-sig))).astype(BF)

def expert(first, slots, at, rows, w_gu, dw, cap, experts, tile=512):
    n=len(rows); J, D2, F = w_gu.shape; D=D2//2; T=rows[0].shape[0]; M=n*cap
    return pl.pallas_call(
        functools.partial(_expert_kernel, count=n, cap=cap, experts=experts),
        grid=(J, F//tile),
        in_specs=[pl.BlockSpec(memory_space=pltpu.SMEM), pl.BlockSpec((n, None, 1, T), lambda j,f:(at,j,0,0))]
          +[pl.BlockSpec((T,D+PAD), lambda j,f:(0,0), pipeline_mode=pl.Buffered(1))]*n
          +[pl.BlockSpec((1,D,tile), lambda j,f:(j,0,f)), pl.BlockSpec((1,D,tile), lambda j,f:(j,1,f)), pl.BlockSpec((1,M,tile), lambda j,f:(j,0,f))],
        out_specs=[pl.BlockSpec((1,M,D), lambda j,f:(j,0,0))]+[pl.BlockSpec((1,M,tile), lambda j,f:(j,0,f))]*3+[pl.BlockSpec((1,M,1), lambda j,f:(j,0,0))],
        out_shape=[jax.ShapeDtypeStruct((J,M,D),BF)]+[jax.ShapeDtypeStruct((J,M,F),BF)]*3+[jax.ShapeDtypeStruct((J,M,1),F32)],
        scratch_shapes=[pltpu.VMEM((M,1),F32)],
        compiler_params=pltpu.CompilerParams(vmem_limit_bytes=VMEM_BYTES),
        cost_estimate=pl.CostEstimate(flops=2*J*M*D*(2*F+T), bytes_accessed=2*(J*D2*F+n*T*D+J*M*(D+4*F)), transcendentals=J*M*F),
        name="expert",
    )(first, slots, *rows, w_gu, w_gu, dw)

def _plus(part, which, more, cols):
    if which is None:
        return part
    more = more[:, cols].astype(F32)
    half = part.shape[0] // 2
    if which == "top":
        return jnp.concatenate([part[:half] + more, part[half:]], axis=0)
    if which == "low":
        return jnp.concatenate([part[:half], part[half:] + more], axis=0)
    return part + more

def _combine_kernel(*refs, terms, count, cap, tile, extra, adds, experts):
    it = iter(refs)
    first = next(it) if extra else None
    slot = next(it)
    factors = [(next(it), next(it)) for _ in range(terms)]
    dgate = next(it) if extra else None
    adds_in = [next(it) if a is not None else None for a in adds]
    outs = [next(it) for _ in range(count)]
    acc = next(it)
    n, j, last = pl.program_id(0), pl.program_id(1), pl.num_programs(1) - 1
    total = None
    for a, w in factors:
        part = dot(a[j], w[0], ((1,),(1,)))
        total = part if total is None else total + part
    total = total.astype(BF)
    cols = pl.ds(pl.multiple_of(n*tile, tile), tile)
    for s in range(count):
        back = pick_back(slot[s, j], cap)
        part = dot(back, total[s*cap:(s+1)*cap], ((1,),(0,)))
        @pl.when(j == 0)
        def _(): acc[s] = _plus(part, adds[s], adds_in[s], cols)
        @pl.when((j > 0) & (j < last))
        def _(): acc[s] += part
        @pl.when(j == last)
        def _(): outs[s][:, cols] = (acc[s] + part).astype(outs[s].dtype)
    if extra:
        D = outs[0].shape[1] - PAD
        @pl.when(n == 0)
        def _():
            lane = lax.broadcasted_iota(jnp.int32, (1, PAD), 1)
            me = first[0] + j
            for s in range(count):
                v = dgate[j, s*cap:(s+1)*cap, :]
                hi = v.astype(BF).astype(F32)
                spread = jnp.where(lane == me, hi, 0.0) + jnp.where(lane == me + experts, v - hi, 0.0)
                part = dot(pick_back(slot[s, j], cap), spread.astype(BF), ((1,),(0,)))
                @pl.when(j == 0)
                def _(): outs[s][:, D:] = _plus(part, adds[s], adds_in[s], slice(D, D + PAD)).astype(outs[s].dtype)
                @pl.when(j > 0)
                def _(): outs[s][:, D:] = (outs[s][:, D:].astype(F32) + part).astype(outs[s].dtype)

def combine(slots, at, factors, cap, adds, first=None, dgate=None, experts=0, tile=1024, out_dtype=BF):
    n = len(adds)
    _, J, T, _ = slots.shape
    M, F = factors[0][0].shape[1:]
    D = factors[-1][1].shape[1] // (factors[-1][2] + 1)
    extra = dgate is not None
    width = D + (PAD if extra else 0)
    steps = D // tile
    one = pl.Buffered(1)
    ops, specs = [], []
    if extra:
        ops.append(first)
        specs.append(pl.BlockSpec(memory_space=pltpu.SMEM))
    ops.append(slots)
    specs.append(pl.BlockSpec((n, J, T, 1), lambda i, j: (at, 0, 0, 0), pipeline_mode=one))
    for a, w, block in factors:
        ops += [a, w]
        specs += [
            pl.BlockSpec((J, M, F), lambda i, j: (0, 0, 0), pipeline_mode=one),
            pl.BlockSpec((1, tile, F), lambda i, j, block=block: (j, block * steps + i, 0)),
        ]
    if extra:
        ops.append(dgate)
        specs.append(pl.BlockSpec((J, M, 1), lambda i, j: (0, 0, 0), pipeline_mode=one))
    for a in adds:
        if a is not None:
            ops.append(a[1])
            specs.append(pl.BlockSpec(a[1].shape, lambda i, j: (0, 0), pipeline_mode=one))
    return pl.pallas_call(
        functools.partial(_combine_kernel, terms=len(factors), count=n, cap=cap, tile=tile, extra=extra, adds=[a and a[0] for a in adds], experts=experts),
        grid=(steps, J),
        in_specs=specs,
        out_specs=[pl.BlockSpec((T, width), lambda i, j: (0, 0))] * n,
        out_shape=[jax.ShapeDtypeStruct((T, width), out_dtype)] * n,
        scratch_shapes=[pltpu.VMEM((n, T, tile), F32)],
        compiler_params=pltpu.CompilerParams(vmem_limit_bytes=VMEM_BYTES),
        cost_estimate=pl.CostEstimate(flops=2 * J * M * D * (len(factors) * F + T), bytes_accessed=2 * len(factors) * J * F * (D + M) + 4 * n * T * D, transcendentals=0),
        name="combine",
    )(*ops)


def _wgrad_kernel(_, *refs, count, pieces):
    xs, gs, outs = refs[:count], refs[count : 2 * count], refs[2 * count :]
    total = None
    for x, g in zip(xs, gs):
        part = dot(x[0], g[0], ((0,), (0,)))
        total = part if total is None else total + part
    for p in range(pieces):

        @pl.when(pl.program_id(2) == p)
        def _(p=p):
            outs[p][0] = total.astype(BF)


def wgrad(order, xs, gs, pieces, tile=2048):
    J, _, D = xs[0].shape
    F = gs[0].shape[2]
    p, n, rows = F // pieces, len(xs), sum(g.shape[1] for g in gs)
    tile = min(tile, D)
    return pl.pallas_call(
        functools.partial(_wgrad_kernel, count=n, pieces=pieces),
        grid=(J, D // tile, pieces),
        in_specs=[pl.BlockSpec(memory_space=pltpu.SMEM)]
        + [pl.BlockSpec((1, x.shape[1], tile), lambda j, i, c: (j, 0, i)) for x in xs]
        + [pl.BlockSpec((1, g.shape[1], p), lambda j, i, c: (j, 0, c)) for g in gs],
        out_specs=[pl.BlockSpec((1, tile, p), lambda j, i, c: (j, i, 0))] * pieces,
        out_shape=[jax.ShapeDtypeStruct((J, D, p), BF)] * pieces,
        compiler_params=pltpu.CompilerParams(vmem_limit_bytes=VMEM_BYTES),
        cost_estimate=pl.CostEstimate(flops=2 * J * rows * D * F, bytes_accessed=2 * J * (rows * (D + F) + D * F), transcendentals=0),
        name="wgrad",
    )(order, *xs, *gs)


def inv_rms(matrix):
    return lax.rsqrt(jnp.mean(matrix * matrix, axis=-1, keepdims=True) + epsilon)


def norm_back(value, gain, grad):
    r = inv_rms(value)
    weighted = gain * grad
    inside = jnp.mean(value * weighted, axis=-1, keepdims=True)
    return r * weighted - value * (r * r * r * inside), jnp.sum(grad * value * r, axis=0)


def angle_tables(positions):
    half_width = HEAD_DIM // 2
    inverse = rope_theta ** (-(jnp.arange(half_width, dtype=F32) * 2.0) / HEAD_DIM)
    angles = positions.astype(F32)[:, None] * inverse[None, :]
    angles = jnp.concatenate([angles, angles], axis=-1)
    sign = jnp.where(jnp.arange(HEAD_DIM) < half_width, -1.0, 1.0)
    return jnp.cos(angles), jnp.sin(angles) * sign


def per_device(
    exp_walk,
    layer_input,
    block_ids,
    routes,
    w_query,
    w_key,
    w_value,
    w_output,
    w_router,
    norm_gains,
    w_gate_up,
    w_down,
    d_out,
):
    C, E = lax.axis_size("ctx"), lax.axis_size("exp")
    c, e = lax.axis_index("ctx"), lax.axis_index("exp")
    Y = C // CORES
    ring = Ring("exp", [exp_walk])
    ctx_ring = Ring("ctx", [[y * CORES + k for y in range(Y)] for k in range(CORES)])
    sibling = [(i, i ^ 1) for i in range(C)]

    def swap(v):
        return lax.ppermute(v, "ctx", sibling)

    def ctx_gather(v):
        got = []
        for block in ctx_ring.gather(v):
            got += [block, swap(block)]
        return got

    def chip_sums(part):
        return [part(dy * CORES).astype(F32) + swap(part(dy * CORES + 1).astype(BF)).astype(F32) for dy in range(Y)]

    def y_sum(mine):
        return ctx_ring.scatter(lambda s: mine[(Y - s) % Y])

    def ctx_sum(rows):
        n = rows.shape[0]
        blocks = jnp.transpose(rows.reshape(n, C, -1), (1, 0, 2))
        whole = jnp.zeros_like(blocks)
        for r in range(C):
            whole = lax.dynamic_update_slice(whole, blocks[r : r + 1], (other_u[r], zero, zero))
        whole = lax.psum(whole, "ctx")
        return jnp.concatenate([lax.dynamic_index_in_dim(whole, other_u[r], 0, False) for r in range(C)], axis=1)

    zero = jnp.uint32(0)
    where = {d: i for i, d in enumerate(exp_walk)}
    left_table = [[exp_walk[(where[i] - s) % E] for s in range(E)] for i in range(E)]
    left_now = lax.dynamic_index_in_dim(jnp.array(left_table, jnp.uint32), e.astype(jnp.uint32), 0, False)
    left_of = [left_now[s] for s in range(E)]

    def put_rows(blocks):
        full = jnp.zeros((E, *blocks[0].shape), BF)
        for s in range(E):
            full = lax.dynamic_update_slice(full, blocks[s][None], (left_of[s], zero, zero))
        return full
    ctx_table = [
        [(i // CORES - r // CORES) % Y * CORES + (i % CORES ^ r % CORES) for r in range(C)] for i in range(C)
    ]
    others = lax.dynamic_index_in_dim(jnp.array(ctx_table, jnp.int32), c.astype(jnp.uint32), 0, False)
    other_u = [others[r].astype(jnp.uint32) for r in range(C)]

    T, D = layer_input.shape[1:]
    rows_e = w_query.shape[0]
    cols_c = D // C
    S = T * C
    half = T // 2
    c_col = (c * cols_c).astype(jnp.uint32)
    NE = w_router.shape[1]
    K = routes.shape[2]
    J = w_gate_up.shape[0]
    cap = (5 * T * K + 4 * NE - 1) // (4 * NE)
    room = -(-cap // 16) * 16
    x = layer_input[0]
    grad_out = d_out[0]

    x_blocks = ctx_gather(x)
    x_all = jnp.concatenate(x_blocks, axis=0)

    small = jnp.concatenate([w_router.reshape(-1), norm_gains.reshape(-1), routes.astype(BF).reshape(-1)])
    small_len = small.shape[0]
    small = jnp.pad(small, (0, -small_len % 4096)).reshape(-1, 128)
    w_qkv_mine = jnp.concatenate(
        [lax.dynamic_slice_in_dim(w, c_col, cols_c, axis=1) for w in (w_query, w_key, w_value)], axis=1
    )
    qkv_walk, small_walk = Gather(ring, w_qkv_mine), Gather(ring, small)
    for _ in range(E // 2):
        small_walk.hop()
        qkv_walk.hop()
        if qkv_walk.count == 2:
            qkv_walk.latest = [v + zero_of(x_blocks[-CORES]).astype(BF) for v in qkv_walk.latest]
        small_walk.latest = [after(v, *qkv_walk.latest) for v in small_walk.latest]
    order = [E // 2, 0] + [i for s in range(1, E // 2) for i in (s, E - s)]
    small_all = jnp.stack([small_walk.got[i] for i in order])
    by_owner = put_rows(small_walk.got)
    cut = rows_e * NE // 128, rows_e * (NE + norm_gains.shape[1]) // 128, small_len // 128
    router_full = by_owner[:, : cut[0]].reshape(D, NE)
    gains = by_owner[:, cut[0] : cut[1]].reshape(D, -1).astype(F32).T
    routes_all = small_all[:, cut[1] : cut[2]].reshape(E, T * K)

    def my_columns(w):
        return lax.dynamic_slice_in_dim(w, c_col, cols_c, axis=1)

    qkv_blocks = qkv_walk.got
    w_qkv = put_rows(qkv_blocks).reshape(D, 3 * cols_c)
    qkv_there = qkv_blocks[E // 2]
    w_out_cols = lax.all_gather(my_columns(w_output), "exp", axis=0, tiled=True)
    w_out_rows = lax.all_to_all(w_out_cols.reshape(C, cols_c, cols_c), "ctx", split_axis=0, concat_axis=0, tiled=True)
    w_out_rows = jnp.transpose(w_out_rows, (1, 0, 2)).reshape(cols_c, D)

    d_walk = Gather(ring, after(grad_out, qkv_there))
    d_walk.hop()
    dn_blocks = ctx_gather(w_down)
    w_dn = jnp.concatenate(dn_blocks, axis=2)

    def hold(v, *others):
        return v + zero_of(*others).astype(v.dtype)

    gu_first = ctx_gather(hold(w_gate_up[: J // 2], dn_blocks[-CORES]))

    blocks_rel = jnp.stack([lax.dynamic_slice_in_dim(block_ids[0], other_u[r] * 2, 2) for r in range(C)]).reshape(-1)
    positions = (blocks_rel[:, None] * half + jnp.arange(half, dtype=jnp.int32)[None, :]).reshape(-1)
    count = jnp.arange(2 * C, dtype=jnp.int32)
    place = jnp.sum(jnp.where(blocks_rel[None, :] == count[:, None], count[None, :], 0), axis=1)
    cosine, sine = angle_tables(positions)
    gain_q = lax.dynamic_slice_in_dim(gains[1:2], c_col, cols_c, axis=1)
    gain_k = lax.dynamic_slice_in_dim(gains[2:3], c_col, cols_c, axis=1)

    groups = [([0], 1)] + [([s, E - s], s) for s in range(1, E // 2)] + [([E // 2], 0)]
    first = (e * J).astype(jnp.int32).reshape(1)
    mine = first[0] + jnp.arange(J, dtype=jnp.int32)
    pairs = (routes_all[:, None, :] == mine[None, :, None].astype(BF)).astype(BF).reshape(E * J, T * K)
    token = jnp.arange(T * K)[:, None] // K
    chosen = dot(pairs, (token == jnp.arange(T)[None, :]).astype(BF), ((1,), (0,)))
    rank = dot(pairs, (token < jnp.arange(T)[None, :]).astype(BF), ((1,), (0,)))
    slot = jnp.where((chosen > 0.5) & (rank < cap), rank, -1.0).astype(jnp.int32).reshape(E, J, T)
    slot_row, slot_col = slot[:, :, None, :], slot[:, :, :, None]

    line, d_slots = Line(), {}

    def fetch(g):
        members, at = groups[g]
        d_slots[g] = dispatch(line.tie(slot_row), at, [d_walk.got[i] for i in members], w_dn, room)
        line.mark(d_slots[g][1])

    fetch(0)
    x_all32 = x_all.astype(F32)
    n1 = (x_all32 * inv_rms(x_all32) * gains[0]).astype(BF)
    qkv = dot(n1, w_qkv, ((1,), (0,)))
    qp, kp = qkv[:, :cols_c], qkv[:, cols_c : 2 * cols_c]
    squares = hold(jnp.stack([jnp.sum(qp * qp, axis=1), jnp.sum(kp * kp, axis=1)]), gu_first[-CORES], d_slots[0][1])
    scales = lax.rsqrt(ctx_sum(squares) / D + epsilon)
    r_q, r_k = scales[0][:, None], scales[1][:, None]
    d_walk.latest = [hold(v, scales) for v in d_walk.latest]
    d_walk.hop()
    gu_last = ctx_gather(hold(w_gate_up[J // 2 :], scales))
    w_gu = lax.optimization_barrier(jnp.concatenate([jnp.concatenate(b, axis=2) for b in (gu_first, gu_last)], axis=0))
    attn, q, k, v, lse = attend(place, qkv, r_q, r_k, cosine, sine, gain_q, gain_k, half)
    branch_part = dot(attn, w_out_rows, ((1,), (0,))).astype(BF)
    chips = chip_sums(lambda r: branch_part[r * T : (r + 1) * T])
    branch = y_sum([hold(v, gu_last[-CORES]) for v in chips])
    d_walk.latest = [hold(v, branch_part) for v in d_walk.latest]
    while d_walk.count < E // 2 - 1:
        d_walk.hop()
    line.mark(branch_part)
    fetch(1)
    branch = hold(branch, w_gu[-1:, -1:, -1:], d_slots[1][1])
    hidden = x.astype(F32) + branch
    n2 = (hidden * inv_rms(hidden) * gains[3]).astype(BF)
    router_own = jax.nn.softmax(dot(n2, router_full, ((1,), (0,))), axis=-1)
    router_high = router_own.astype(BF)
    router_low = (router_own - router_high.astype(F32)).astype(BF)
    n2_wide = jnp.concatenate([n2, router_high, router_low, jnp.zeros((T, PAD - 2 * NE), BF)], axis=1)

    line, n2_walk, done = Line(), Gather(ring, n2_wide), {}

    def work(g):
        members, at = groups[g]
        done[g] = expert(first, line.tie(slot_row), at, [n2_walk.got[i] for i in members], w_gu, d_slots[g][1], room, NE)
        line.mark(done[g][1])

    def back(g):
        members, at = groups[g]
        _, dg, du, _, dgate = done[g]
        kind = F32 if members == [0] else BF
        got = combine(line.tie(slot_col), at, [(dg, w_gu, 0), (du, w_gu, 1)], room, [None] * len(members), first, dgate, NE, out_dtype=kind)
        line.mark(got[0])
        return got

    def mix(g):
        members, at = groups[g]
        kind = F32 if members == [0] else BF
        got = combine(line.tie(slot_col), at, [(done[g][3], w_dn, 0)], room, [None] * len(members), out_dtype=kind)
        line.mark(got[0])
        return got

    def grads(left, right):
        parts = wgrad(line.zero(), left, right, C)
        line.mark(parts[0])
        return chip_sums(lambda r: parts[r])

    far = E // 2
    n2_walk.hop()
    line.mark(n2_wide)
    work(0)
    d_walk.latest = [hold(v, done[0][1]) for v in d_walk.latest]
    d_walk.hop()
    fetch(2)
    for g in range(1, far + 1):
        line.mark(*n2_walk.latest, line.last[0])
        if g < far:
            n2_walk.hop()
        work(g)
        if g + 1 < far:
            fetch(g + 2)
    home = Home(ring, back(far)[0])
    for g in range(far - 1, 0, -1):
        terms = back(g)
        line.mark(*home.arrived, line.last[0])
        home.hop(*terms)
    [own] = back(0)
    chips_g = grads([done[i][0] for i in done], [done[i][1] for i in done])
    [mix_far] = mix(far)
    line.mark(*home.arrived, line.last[0])
    rows_back = own + home.arrived[0].astype(F32) + home.arrived[1].astype(F32)
    mixed = Home(ring, after(mix_far, *home.arrived))
    drouter = rows_back[:, D : D + NE] + rows_back[:, D + NE : D + 2 * NE]
    dlogits = (router_own * (drouter - jnp.sum(drouter * router_own, axis=-1, keepdims=True))).astype(BF)
    dn2 = rows_back[:, :D] + dot(dlogits, router_full, ((1,), (1,)))
    hidden_part, d_gain3 = norm_back(hidden, gains[3], dn2)
    dhidden = grad_out.astype(F32) + hidden_part
    dhidden_low = dhidden.astype(BF)
    dhidden_blocks = ctx_gather(dhidden_low)
    dhidden_all = jnp.concatenate(dhidden_blocks, axis=0)
    line.mark(dhidden_low)
    terms = {}
    for g in range(far - 1, -1, -1):
        terms[g] = mix(g)
        if g == far - 1:
            line.mark(*mixed.arrived, line.last[0])
            mixed.hop(*terms[g])
            line.mark(*terms[g])
            chips_u = grads([done[i][0] for i in done], [done[i][2] for i in done])
    sum_g = y_sum([hold(v, dhidden_blocks[-CORES]) for v in chips_g])

    def pump():
        if mixed.near > 1:
            line.mark(*mixed.arrived, *line.last)
            mixed.hop(*terms[mixed.near - 1])

    dattn = dot(after(dhidden_all, *line.last), w_out_rows, ((1,), (1,))).astype(BF)
    g_out = dot(attn, dhidden_all, ((0,), (0,))).astype(BF)
    line.mark(g_out, dattn)
    pump()
    wq, wk, dv, inside, d_gain_qk = attend_back(line.tie(place), q, k, v, dattn, lse, qkv, r_q, r_k, cosine, sine, gain_q, gain_k, half)
    line.mark(dv)
    pump()
    def next_hop(walk, of):
        if walk.near > 1:
            line.mark(*walk.arrived, *line.last)
            walk.hop(of(walk.near - 1), of(E - walk.near + 1))

    g_out = jnp.transpose(g_out.reshape(cols_c, C, cols_c), (1, 0, 2))
    g_out = lax.all_to_all(g_out, "ctx", split_axis=0, concat_axis=0, tiled=True).reshape(E, rows_e, cols_c)
    g_router = dot(dlogits, n2, ((0,), (0,)))
    spread = lax.dynamic_update_slice(jnp.zeros((2, D), F32), d_gain_qk, (zero, c_col))
    g_small = jnp.concatenate([g_router, spread, d_gain3[None]], axis=0)
    count = g_small.shape[0]
    g_small = jnp.transpose(g_small.reshape(count, E, rows_e), (1, 0, 2)).reshape(E, -1)
    unit = 3 * 16
    small_rows = -(-(rows_e * cols_c + count * rows_e) // (cols_c * unit)) * unit - rows_e
    g_small = jnp.pad(g_small, ((0, 0), (0, small_rows * cols_c - count * rows_e))).reshape(E, small_rows, cols_c)
    more = jnp.concatenate([g_out, g_small.astype(BF)], axis=1).reshape(E, -1, 3 * cols_c)
    more = lax.optimization_barrier(more)

    inside = ctx_sum(hold(line.tie(inside)[:, :2].T, sum_g, more)) / D
    dqp = r_q * wq - qp * (r_q * r_q * r_q * inside[0][:, None])
    dkp = r_k * wk - kp * (r_k * r_k * r_k * inside[1][:, None])
    dqkv = jnp.concatenate([dqp.astype(BF), dkp.astype(BF), dv], axis=1)
    g_qkv = dot(n1, dqkv, ((0,), (0,))).astype(BF).reshape(E, rows_e, 3 * cols_c)

    def of_qkv(s):
        return jnp.concatenate([lax.dynamic_index_in_dim(a, left_of[s], 0, False) for a in (g_qkv, more)], axis=0)

    qkv_home = Home(ring, of_qkv(far))
    sum_u = y_sum([hold(v, inside) for v in chips_u])
    line.mark(g_qkv)
    dn1_part = dot(line.tie(dqkv), w_qkv, ((1,), (1,))).astype(BF)
    line.mark(dn1_part)
    next_hop(qkv_home, lambda s: hold(of_qkv(s), sum_u))
    chips_n1 = chip_sums(lambda r: dn1_part[r * T : (r + 1) * T])
    dn1 = y_sum(chips_n1)
    next_hop(qkv_home, of_qkv)
    line.mark(*qkv_home.sent, *mixed.arrived)
    chips_d = grads([d_slots[i][0] for i in done], [done[i][3] for i in done])
    sum_d = y_sum(chips_d)

    def arrived_sum(walk, own):
        return own.astype(F32) + walk.arrived[0].astype(F32) + walk.arrived[1].astype(F32)

    while qkv_home.near > 1:
        next_hop(qkv_home, lambda s: hold(of_qkv(s), sum_d))
    x32 = x.astype(F32)
    token_part, _ = norm_back(x32, gains[0], dn1)
    d_x = (dhidden + token_part)[None]
    g_gate_up = jnp.concatenate([sum_g, sum_u], axis=1)
    g_down = sum_d
    while mixed.near > 1:
        pump()
    output = (hidden + terms[0][0] + mixed.arrived[0].astype(F32) + mixed.arrived[1].astype(F32)).astype(BF)[None]

    dense_mine = arrived_sum(qkv_home, of_qkv(0))
    g_qkv_mine = dense_mine[:rows_e]
    own_gain = norm_gains[:, 0].astype(F32)
    d_gain0 = jnp.sum(w_qkv_mine.astype(F32) * g_qkv_mine, axis=1) / own_gain
    gain_rows = -(-rows_e // (3 * cols_c * 16)) * 16
    d_gain0 = jnp.pad(d_gain0, (0, gain_rows * 3 * cols_c - rows_e)).reshape(gain_rows, 3 * cols_c)
    pieces = ctx_gather(jnp.concatenate([dense_mine, d_gain0], axis=0).astype(BF))
    g_query, g_key, g_value = columns(others, pieces, rows_e, cols_c)
    last = dense_mine.shape[0]
    out_pieces = [p[rows_e:last].reshape(-1, cols_c) for p in pieces]
    [g_output] = columns(others, out_pieces, rows_e, cols_c)
    g_small = sum(p[rows_e:].astype(F32) for p in out_pieces).reshape(-1)[: count * rows_e].reshape(count, rows_e)
    d_gain0 = sum(p[last:].astype(F32) for p in pieces).reshape(-1)[:rows_e]
    g_gains = jnp.concatenate([d_gain0[None], g_small[NE:]], axis=0).T
    return (output, d_x, g_query, g_key, g_value, g_output, g_small[:NE].T, g_gains, g_gate_up, g_down)


def solution(mesh):
    exp_walk = ring_order(mesh.shape["exp"])
    tokens = P("exp", "ctx", None)
    rows = P("exp", None)
    hidden_units = P("exp", None, "ctx")
    in_specs = (tokens, rows, tokens) + (rows,) * 6 + (hidden_units, hidden_units, tokens)
    out_specs = (tokens, tokens) + (rows,) * 6 + (hidden_units, hidden_units)
    return jax.shard_map(
        functools.partial(per_device, exp_walk),
        mesh=mesh,
        in_specs=in_specs,
        out_specs=out_specs,
        check_vma=False,
    )
```

```python
import functools

import jax
import jax.numpy as jnp
from jax import lax
from jax.experimental import pallas as pl
from jax.experimental.pallas import tpu as pltpu
from jax.sharding import PartitionSpec as P

HEAD_DIM = 128
CORES = 2
ROWS_Z = 4
VMEM_BYTES = 56 << 20

epsilon = 1e-05
rope_theta = 10000.0
BF = jnp.bfloat16
F32 = jnp.float32


def dot(a, b, dims):
    return lax.dot_general(a, b, (dims, ((), ())), preferred_element_type=F32)


def after(v, *others):
    return lax.optimization_barrier((v, *others))[0]


def zero_of(*arrays):
    return sum(a[(0,) * a.ndim].astype(F32) for a in arrays) * 0.0


def ring_order(count):
    rows = ROWS_Z if count % ROWS_Z == 0 else 1
    across = count // rows
    walk = [(0, 0)]
    for z in range(rows):
        xs = range(1, across)
        walk += [(z, x) for x in (xs if z % 2 == 0 else reversed(xs))]
    walk += [(z, 0) for z in range(rows - 1, 0, -1)]
    return [z * across + x for z, x in walk]


class Ring:
    def __init__(self, axis, rings):
        self.axis = axis
        self.size = len(rings[0])
        self.right = [
            (r[i], r[(i + 1) % self.size]) for r in rings for i in range(self.size)
        ]
        self.left = [(b, a) for a, b in self.right]

    def go_right(self, v):
        return lax.ppermute(v, self.axis, self.right)

    def go_left(self, v):
        return lax.ppermute(v, self.axis, self.left)

    def gather(self, v):
        if self.size == 2:
            return [v, self.go_right(v)]
        walk = Gather(self, v)
        for _ in range(self.size // 2):
            walk.hop()
        return walk.got

    def scatter(self, part, dtype=BF):
        n = self.size
        far = part(n // 2).astype(dtype)
        if n == 2:
            return part(0) + self.go_right(far).astype(F32)
        half = far.shape[0] // 2
        from_left = self.go_right(far[:half]).astype(F32)
        from_right = self.go_left(far[half:]).astype(F32)
        from_left = jnp.concatenate([from_left, jnp.zeros_like(from_left)], axis=0)
        from_right = jnp.concatenate([jnp.zeros_like(from_right), from_right], axis=0)
        for s in range(n // 2 - 1, 0, -1):
            to_right = (part(s) + from_left).astype(dtype)
            to_left = (part(n - s) + from_right).astype(dtype)
            from_left = self.go_right(to_right).astype(F32)
            from_right = self.go_left(to_left).astype(F32)
        return part(0) + from_left + from_right

class Home:
    def __init__(self, ring, far):
        half = far.shape[0] // 2
        self.ring, self.near, self.half = ring, ring.size // 2, half
        self.arrived = ring.go_right(far[:half]), ring.go_left(far[half:])

    def hop(self, to_left, to_right):
        left, right = self.arrived
        if self.near == self.ring.size // 2:
            to_right = jnp.concatenate([to_right[: self.half] + left, to_right[self.half :]], axis=0)
            to_left = jnp.concatenate([to_left[: self.half], to_left[self.half :] + right], axis=0)
        else:
            to_right, to_left = to_right + left, to_left + right
        self.near -= 1
        self.sent = to_right, to_left
        self.arrived = self.ring.go_right(to_right), self.ring.go_left(to_left)


class Line:
    def __init__(self):
        self.last = ()

    def mark(self, *arrays):
        self.last = arrays

    def tie(self, v):
        return after(v, *self.last) if self.last else v

    def zero(self):
        return zero_of(*self.last).astype(jnp.int32).reshape(1)


class Gather:
    def __init__(self, ring, v):
        self.ring, self.count = ring, 0
        self.got = [v] + [None] * (ring.size - 1)
        self.latest = (v, v)

    def hop(self):
        n, (right, left) = self.ring.size, self.latest
        self.count += 1
        s = self.count
        if s < n // 2:
            self.latest = self.ring.go_right(right), self.ring.go_left(left)
            self.got[s], self.got[n - s] = self.latest
        elif s == n // 2:
            half = right.shape[0] // 2
            self.latest = self.ring.go_right(right[:half]), self.ring.go_left(left[half:])
            self.got[s] = jnp.concatenate(self.latest, axis=0)


def _scores(q, k, row0, scale):
    raw = dot(q, k, ((1,), (1,))) * scale
    rows = lax.broadcasted_iota(jnp.int32, raw.shape, 0) + row0
    cols = lax.broadcasted_iota(jnp.int32, raw.shape, 1)
    return jnp.where(cols <= rows, raw, -1e30)


def _turn(v, cosine, sine):
    return v * cosine + pltpu.roll(v, HEAD_DIM // 2, 1) * sine


def _attend_kernel(place, qp, kp, vp, rq, rk, cosine, sine, gq, gk, o_ref, q_s, k_s, v_s, lse_ref, o_s, *, half, blocks, tile, scale):
    for b in range(blocks):
        at, to = pl.ds(pl.multiple_of(place[b] * half, half), half), slice(b * half, (b + 1) * half)
        c, s = cosine[at, :], sine[at, :]
        q_s[to, :] = _turn(qp[at, :] * rq[at, :] * gq[...], c, s).astype(BF)
        k_s[to, :] = _turn(kp[at, :] * rk[at, :] * gk[...], c, s).astype(BF)
        v_s[to, :] = vp[at, :].astype(BF)
    for i in range(half * blocks // tile):
        width = (i + 1) * tile
        s = _scores(q_s[i * tile : width, :], k_s[:width, :], i * tile, scale)
        top = jnp.max(s, axis=-1, keepdims=True)
        total = top + jnp.log(jnp.sum(jnp.exp(s - top), axis=-1, keepdims=True))
        p = jnp.exp(s - total).astype(BF)
        o_s[i * tile : width, :] = dot(p, v_s[:width, :], ((1,), (0,))).astype(BF)
        lse_ref[0, i * tile : width, :] = total
    for b in range(blocks):
        at = pl.multiple_of(place[b] * half, half)
        o_ref[pl.ds(at, half), :] = o_s[b * half : (b + 1) * half, :]


def _attend_back_kernel(place, q_s, k_s, v_s, d_ref, lse_ref, qp, kp, rq, rk, cosine, sine, gq, gk, wq_ref, wk_ref, dv_ref, in_ref, gain_ref,
                        d_s, dq_s, dk_s, dv_s, *, half, blocks, tile, scale):
    for b in range(blocks):
        at = pl.ds(pl.multiple_of(place[b] * half, half), half)
        d_s[b * half : (b + 1) * half, :] = d_ref[at, :]
    count = half * blocks // tile
    for i in reversed(range(count)):
        width = (i + 1) * tile
        here = slice(i * tile, width)
        q, d, k, v = q_s[here, :], d_s[here, :], k_s[:width, :], v_s[:width, :]
        p = jnp.exp(_scores(q, k, i * tile, scale) - lse_ref[0, here, :])
        dp = dot(d, v, ((1,), (1,)))
        row = jnp.sum(p * dp, axis=-1, keepdims=True)
        ds = (p * (dp - row)).astype(BF)
        dq_s[here, :] = dot(ds, k, ((1,), (0,)))
        dk = dot(ds, q, ((0,), (0,)))
        dv = dot(p.astype(BF), d, ((0,), (0,)))
        if i == count - 1:
            dk_s[:width, :] = dk
            dv_s[:width, :] = dv
        else:
            dk_s[:width, :] += dk
            dv_s[:width, :] += dv

    @pl.when(pl.program_id(0) == 0)
    def _():
        in_ref[...] = jnp.zeros_like(in_ref)

    sums = [jnp.zeros((1, HEAD_DIM), F32)] * 2
    lane = lax.broadcasted_iota(jnp.int32, (1, in_ref.shape[1]), 1)
    for b in range(blocks):
        at, here = pl.ds(pl.multiple_of(place[b] * half, half), half), slice(b * half, (b + 1) * half)
        c, s = cosine[at, :], sine[at, :]
        for n, (grad, pre, r, gain, out) in enumerate(((dq_s, qp, rq, gq, wq_ref), (dk_s, kp, rk, gk, wk_ref))):
            t = _turn(grad[here, :] * scale, c, -s)
            value = pre[at, :]
            w = t * gain[...]
            out[at, :] = w
            in_ref[at, :] += jnp.where(lane == n, jnp.sum(value * w, axis=-1, keepdims=True), 0.0)
            sums[n] = sums[n] + jnp.sum(t * value * r[at, :], axis=0, keepdims=True)
        dv_ref[at, :] = dv_s[here, :].astype(BF)
    gain_ref[0:1, :] = sums[0]
    gain_ref[1:2, :] = sums[1]


def _head_specs(rows, heads):
    head = lambda k: pl.BlockSpec((rows, HEAD_DIM), lambda h, place: (0, k * heads + h))
    lse = pl.BlockSpec((1, rows, 1), lambda h, place: (h, 0, 0))
    col = pl.BlockSpec((rows, 1), lambda h, place: (0, 0))
    table = pl.BlockSpec((rows, HEAD_DIM), lambda h, place: (0, 0))
    gain = pl.BlockSpec((1, HEAD_DIM), lambda h, place: (0, h))
    return head, lse, col, table, gain


def _sizes(rows, half):
    return dict(half=half, blocks=rows // half, tile=min(384, rows), scale=HEAD_DIM**-0.5)


def attend(place, qkv, rq, rk, cosine, sine, gq, gk, half):
    rows, width = qkv.shape[0], qkv.shape[1] // 3
    heads = width // HEAD_DIM
    head, lse, col, table, gain = _head_specs(rows, heads)
    return pl.pallas_call(
        functools.partial(_attend_kernel, **_sizes(rows, half)),
        grid_spec=pltpu.PrefetchScalarGridSpec(
            num_scalar_prefetch=1,
            grid=(heads,),
            in_specs=[head(0), head(1), head(2), col, col, table, table, gain, gain],
            out_specs=[head(0)] * 4 + [lse],
            scratch_shapes=[pltpu.VMEM((rows, HEAD_DIM), BF)],
        ),
        out_shape=[jax.ShapeDtypeStruct((rows, width), BF)] * 4 + [jax.ShapeDtypeStruct((heads, rows, 1), F32)],
        compiler_params=pltpu.CompilerParams(vmem_limit_bytes=VMEM_BYTES),
        cost_estimate=pl.CostEstimate(flops=2 * rows * rows * width * 2, bytes_accessed=20 * rows * width, transcendentals=heads * rows * rows),
        name="attend",
    )(place, qkv, qkv, qkv, rq, rk, cosine, sine, gq, gk)


def attend_back(place, q, k, v, d, lse_in, qkv, rq, rk, cosine, sine, gq, gk, half):
    rows, width = q.shape
    heads = width // HEAD_DIM
    head, lse, col, table, gain = _head_specs(rows, heads)
    return pl.pallas_call(
        functools.partial(_attend_back_kernel, **_sizes(rows, half)),
        grid_spec=pltpu.PrefetchScalarGridSpec(
            num_scalar_prefetch=1,
            grid=(heads,),
            in_specs=[head(0)] * 4 + [lse, head(0), head(1), col, col, table, table, gain, gain],
            out_specs=[head(0)] * 3
            + [pl.BlockSpec((rows, 8), lambda h, place: (0, 0)), pl.BlockSpec((2, HEAD_DIM), lambda h, place: (0, h))],
            scratch_shapes=[pltpu.VMEM((rows, HEAD_DIM), BF)] + [pltpu.VMEM((rows, HEAD_DIM), F32)] * 3,
        ),
        out_shape=[
            jax.ShapeDtypeStruct((rows, width), F32),
            jax.ShapeDtypeStruct((rows, width), F32),
            jax.ShapeDtypeStruct((rows, width), BF),
            jax.ShapeDtypeStruct((rows, 8), F32),
            jax.ShapeDtypeStruct((2, width), F32),
        ],
        compiler_params=pltpu.CompilerParams(vmem_limit_bytes=VMEM_BYTES),
        cost_estimate=pl.CostEstimate(flops=5 * rows * rows * width * 2, bytes_accessed=28 * rows * width, transcendentals=heads * rows * rows),
        name="attend_back",
    )(place, q, k, v, d, lse_in, qkv, qkv, rq, rk, cosine, sine, gq, gk)


def _columns_kernel(place, *refs, pieces, weights, cols):
    for r in range(pieces):
        at = pl.ds(pl.multiple_of(place[r] * cols, cols), cols)
        for w in range(weights):
            refs[pieces + w][:, at] = refs[r][:, w * cols : (w + 1) * cols].astype(F32)


def columns(place, blocks, rows, cols):
    n, tile = len(blocks), min(rows, 64)
    weights = blocks[0].shape[1] // cols
    return pl.pallas_call(
        functools.partial(_columns_kernel, pieces=n, weights=weights, cols=cols),
        grid_spec=pltpu.PrefetchScalarGridSpec(
            num_scalar_prefetch=1,
            grid=(rows // tile,),
            in_specs=[pl.BlockSpec((tile, weights * cols), lambda i, place: (i, 0))] * n,
            out_specs=[pl.BlockSpec((tile, n * cols), lambda i, place: (i, 0))] * weights,
        ),
        out_shape=[jax.ShapeDtypeStruct((rows, n * cols), F32)] * weights,
        compiler_params=pltpu.CompilerParams(vmem_limit_bytes=VMEM_BYTES),
        name="columns",
    )(place, *blocks)


PAD=128

def pick_rows(slot_row, cap):
    return (lax.broadcasted_iota(jnp.int32, (cap, slot_row.shape[1]), 0) == slot_row).astype(BF)

def pick_back(slot_col, cap):
    return (lax.broadcasted_iota(jnp.int32, (slot_col.shape[0], cap), 1) == slot_col).astype(BF)

def _dispatch_kernel(*refs, count, cap):
    slot, rows, w, out_x, out_w = refs[0], refs[1:1+count], refs[1+count], refs[2+count], refs[3+count]
    @pl.when(pl.program_id(1) == 0)
    def _():
        for s in range(count):
            out_x[0, s*cap:(s+1)*cap, :] = dot(pick_rows(slot[s], cap), rows[s][...], ((1,),(0,))).astype(BF)
    out_w[0] = dot(out_x[0], w[0], ((1,),(0,))).astype(BF)

def dispatch(slots, at, rows, w, cap, tile=512):
    n, (J, D, F), T = len(rows), w.shape, rows[0].shape[0]
    M = n * cap
    return pl.pallas_call(
        functools.partial(_dispatch_kernel, count=n, cap=cap),
        grid=(J, F // tile),
        in_specs=[pl.BlockSpec((n, None, 1, T), lambda j, f: (at, j, 0, 0))]
        + [pl.BlockSpec((T, D), lambda j, f: (0, 0), pipeline_mode=pl.Buffered(1))] * n
        + [pl.BlockSpec((1, D, tile), lambda j, f: (j, 0, f))],
        out_specs=[pl.BlockSpec((1, M, D), lambda j, f: (j, 0, 0)), pl.BlockSpec((1, M, tile), lambda j, f: (j, 0, f))],
        out_shape=[jax.ShapeDtypeStruct((J, M, D), BF), jax.ShapeDtypeStruct((J, M, F), BF)],
        compiler_params=pltpu.CompilerParams(vmem_limit_bytes=VMEM_BYTES),
        cost_estimate=pl.CostEstimate(flops=2 * J * M * D * (F + T), bytes_accessed=2 * (J * D * F + n * T * D + J * M * (D + F)), transcendentals=0),
        name="dispatch",
    )(slots, *rows, w)


def _expert_kernel(first, slot, *refs, count, cap, experts):
    rows = refs[:count]
    wg, wu, dw, out_x, out_dg, out_du, out_in, out_dgate, gate = refs[count:]
    D = wg.shape[1]
    f = pl.program_id(1)
    @pl.when(f == 0)
    def _():
        mine = lax.broadcasted_iota(jnp.int32, (1, PAD), 1)
        me = first[0] + pl.program_id(0)
        mask = ((mine == me) | (mine == me + experts)).astype(F32)
        for s in range(count):
            at = slice(s*cap,(s+1)*cap)
            got = dot(pick_rows(slot[s], cap), rows[s][...], ((1,),(0,)))
            out_x[0, at, :] = got[:, :D].astype(BF)
            gate[at, :] = jnp.sum(got[:, D:]*mask, axis=-1, keepdims=True)
        out_dgate[...] = jnp.zeros_like(out_dgate)
    x = out_x[0]
    g = dot(x, wg[0], ((1,),(0,)))
    u = dot(x, wu[0], ((1,),(0,)))
    sig = 1.0/(1.0+jnp.exp(-g))
    act = g*sig
    inner = act*u
    d = dw[0].astype(F32)
    out_dgate[0] += jnp.sum(inner*d, axis=-1, keepdims=True)
    scaled = gate[...]
    d = d*scaled
    out_in[0] = (inner*scaled).astype(BF)
    out_du[0] = (d*act).astype(BF)
    out_dg[0] = (d*u*(sig + act*(1.0-sig))).astype(BF)

def expert(first, slots, at, rows, w_gu, dw, cap, experts, tile=512):
    n=len(rows); J, D2, F = w_gu.shape; D=D2//2; T=rows[0].shape[0]; M=n*cap
    return pl.pallas_call(
        functools.partial(_expert_kernel, count=n, cap=cap, experts=experts),
        grid=(J, F//tile),
        in_specs=[pl.BlockSpec(memory_space=pltpu.SMEM), pl.BlockSpec((n, None, 1, T), lambda j,f:(at,j,0,0))]
          +[pl.BlockSpec((T,D+PAD), lambda j,f:(0,0), pipeline_mode=pl.Buffered(1))]*n
          +[pl.BlockSpec((1,D,tile), lambda j,f:(j,0,f)), pl.BlockSpec((1,D,tile), lambda j,f:(j,1,f)), pl.BlockSpec((1,M,tile), lambda j,f:(j,0,f))],
        out_specs=[pl.BlockSpec((1,M,D), lambda j,f:(j,0,0))]+[pl.BlockSpec((1,M,tile), lambda j,f:(j,0,f))]*3+[pl.BlockSpec((1,M,1), lambda j,f:(j,0,0))],
        out_shape=[jax.ShapeDtypeStruct((J,M,D),BF)]+[jax.ShapeDtypeStruct((J,M,F),BF)]*3+[jax.ShapeDtypeStruct((J,M,1),F32)],
        scratch_shapes=[pltpu.VMEM((M,1),F32)],
        compiler_params=pltpu.CompilerParams(vmem_limit_bytes=VMEM_BYTES),
        cost_estimate=pl.CostEstimate(flops=2*J*M*D*(2*F+T), bytes_accessed=2*(J*D2*F+n*T*D+J*M*(D+4*F)), transcendentals=J*M*F),
        name="expert",
    )(first, slots, *rows, w_gu, w_gu, dw)

def _plus(part, which, more, cols):
    if which is None:
        return part
    more = more[:, cols].astype(F32)
    half = part.shape[0] // 2
    if which == "top":
        return jnp.concatenate([part[:half] + more, part[half:]], axis=0)
    if which == "low":
        return jnp.concatenate([part[:half], part[half:] + more], axis=0)
    return part + more

def _combine_kernel(*refs, terms, count, cap, tile, extra, adds, experts):
    it = iter(refs)
    first = next(it)
    slot = next(it)
    factors = [(next(it), next(it)) for _ in range(terms)]
    dgate = next(it) if extra else None
    adds_in = [next(it) if a is not None else None for a in adds]
    outs = [next(it) for _ in range(count)]
    acc = next(it)
    n, j, last = pl.program_id(0), pl.program_id(1), pl.num_programs(1) - 1
    total = None
    for a, w in factors:
        part = dot(a[j], w[0], ((1,),(1,)))
        total = part if total is None else total + part
    total = total.astype(BF)
    cols = pl.ds(pl.multiple_of(n*tile, tile), tile)
    for s in range(count):
        back = pick_back(slot[s, j], cap)
        part = dot(back, total[s*cap:(s+1)*cap], ((1,),(0,)))
        @pl.when(j == 0)
        def _(): acc[s] = _plus(part, adds[s], adds_in[s], cols)
        @pl.when((j > 0) & (j < last))
        def _(): acc[s] += part
        @pl.when(j == last)
        def _(): outs[s][:, cols] = (acc[s] + part).astype(outs[s].dtype)
    if extra:
        D = outs[0].shape[1] - PAD
        @pl.when(n == 0)
        def _():
            lane = lax.broadcasted_iota(jnp.int32, (1, PAD), 1)
            me = first[0] + j
            for s in range(count):
                v = dgate[j, s*cap:(s+1)*cap, :]
                hi = v.astype(BF).astype(F32)
                spread = jnp.where(lane == me, hi, 0.0) + jnp.where(lane == me + experts, v - hi, 0.0)
                part = dot(pick_back(slot[s, j], cap), spread.astype(BF), ((1,),(0,)))
                @pl.when(j == 0)
                def _(): outs[s][:, D:] = _plus(part, adds[s], adds_in[s], slice(D, D + PAD)).astype(outs[s].dtype)
                @pl.when(j > 0)
                def _(): outs[s][:, D:] = (outs[s][:, D:].astype(F32) + part).astype(outs[s].dtype)

def combine(slots, at, factors, cap, adds, first, dgate=None, experts=0, tile=1024, out_dtype=BF):
    n = len(adds)
    _, J, T, _ = slots.shape
    M, F = factors[0][0].shape[1:]
    D = factors[-1][1].shape[1] // (factors[-1][2] + 1)
    extra = dgate is not None
    width = D + (PAD if extra else 0)
    steps = D // tile
    one = pl.Buffered(1)
    ops, specs = [first], [pl.BlockSpec(memory_space=pltpu.SMEM)]
    ops.append(slots)
    specs.append(pl.BlockSpec((n, J, T, 1), lambda i, j: (at, 0, 0, 0), pipeline_mode=one))
    for a, w, block in factors:
        ops += [a, w]
        specs += [
            pl.BlockSpec((J, M, F), lambda i, j: (0, 0, 0), pipeline_mode=one),
            pl.BlockSpec((1, tile, F), lambda i, j, block=block: (j, block * steps + i, 0)),
        ]
    if extra:
        ops.append(dgate)
        specs.append(pl.BlockSpec((J, M, 1), lambda i, j: (0, 0, 0), pipeline_mode=one))
    for a in adds:
        if a is not None:
            ops.append(a[1])
            specs.append(pl.BlockSpec(a[1].shape, lambda i, j: (0, 0), pipeline_mode=one))
    return pl.pallas_call(
        functools.partial(_combine_kernel, terms=len(factors), count=n, cap=cap, tile=tile, extra=extra, adds=[a and a[0] for a in adds], experts=experts),
        grid=(steps, J),
        in_specs=specs,
        out_specs=[pl.BlockSpec((T, width), lambda i, j: (0, 0))] * n,
        out_shape=[jax.ShapeDtypeStruct((T, width), out_dtype)] * n,
        scratch_shapes=[pltpu.VMEM((n, T, tile), F32)],
        compiler_params=pltpu.CompilerParams(vmem_limit_bytes=VMEM_BYTES),
        cost_estimate=pl.CostEstimate(flops=2 * J * M * D * (len(factors) * F + T), bytes_accessed=2 * len(factors) * J * F * (D + M) + 4 * n * T * D, transcendentals=0),
        name="combine",
    )(*ops)


def _wgrad_kernel(_, *refs, count, pieces):
    xs, gs, outs = refs[:count], refs[count : 2 * count], refs[2 * count :]
    total = None
    for x, g in zip(xs, gs):
        part = dot(x[0], g[0], ((0,), (0,)))
        total = part if total is None else total + part
    for p in range(pieces):

        @pl.when(pl.program_id(2) == p)
        def _(p=p):
            outs[p][0] = total.astype(BF)


def wgrad(order, xs, gs, pieces, tile=2048):
    J, _, D = xs[0].shape
    F = gs[0].shape[2]
    p, n, rows = F // pieces, len(xs), sum(g.shape[1] for g in gs)
    tile = min(tile, D)
    return pl.pallas_call(
        functools.partial(_wgrad_kernel, count=n, pieces=pieces),
        grid=(J, D // tile, pieces),
        in_specs=[pl.BlockSpec(memory_space=pltpu.SMEM)]
        + [pl.BlockSpec((1, x.shape[1], tile), lambda j, i, c: (j, 0, i)) for x in xs]
        + [pl.BlockSpec((1, g.shape[1], p), lambda j, i, c: (j, 0, c)) for g in gs],
        out_specs=[pl.BlockSpec((1, tile, p), lambda j, i, c: (j, i, 0))] * pieces,
        out_shape=[jax.ShapeDtypeStruct((J, D, p), BF)] * pieces,
        compiler_params=pltpu.CompilerParams(vmem_limit_bytes=VMEM_BYTES),
        cost_estimate=pl.CostEstimate(flops=2 * J * rows * D * F, bytes_accessed=2 * J * (rows * (D + F) + D * F), transcendentals=0),
        name="wgrad",
    )(order, *xs, *gs)


def inv_rms(matrix):
    return lax.rsqrt(jnp.mean(matrix * matrix, axis=-1, keepdims=True) + epsilon)


def norm_back(value, gain, grad):
    r = inv_rms(value)
    weighted = gain * grad
    inside = jnp.mean(value * weighted, axis=-1, keepdims=True)
    return r * weighted - value * (r * r * r * inside), jnp.sum(grad * value * r, axis=0)


def angle_tables(positions):
    half_width = HEAD_DIM // 2
    inverse = rope_theta ** (-(jnp.arange(half_width, dtype=F32) * 2.0) / HEAD_DIM)
    angles = positions.astype(F32)[:, None] * inverse[None, :]
    angles = jnp.concatenate([angles, angles], axis=-1)
    sign = jnp.where(jnp.arange(HEAD_DIM) < half_width, -1.0, 1.0)
    return jnp.cos(angles), jnp.sin(angles) * sign


def per_device(
    exp_walk,
    layer_input,
    block_ids,
    routes,
    w_query,
    w_key,
    w_value,
    w_output,
    w_router,
    norm_gains,
    w_gate_up,
    w_down,
    d_out,
):
    C, E = lax.axis_size("ctx"), lax.axis_size("exp")
    c, e = lax.axis_index("ctx"), lax.axis_index("exp")
    Y = C // CORES
    ring = Ring("exp", [exp_walk])
    ctx_ring = Ring("ctx", [[y * CORES + k for y in range(Y)] for k in range(CORES)])
    sibling = [(i, i ^ 1) for i in range(C)]

    def swap(v):
        return lax.ppermute(v, "ctx", sibling)

    def ctx_gather(v):
        got = []
        for block in ctx_ring.gather(v):
            got += [block, swap(block)]
        return got

    def chip_sums(part):
        return [part(dy * CORES).astype(F32) + swap(part(dy * CORES + 1).astype(BF)).astype(F32) for dy in range(Y)]

    def y_sum(mine):
        return ctx_ring.scatter(lambda s: mine[(Y - s) % Y])

    def ctx_sum(rows):
        n = rows.shape[0]
        blocks = jnp.transpose(rows.reshape(n, C, -1), (1, 0, 2))
        whole = jnp.zeros_like(blocks)
        for r in range(C):
            whole = lax.dynamic_update_slice(whole, blocks[r : r + 1], (other_u[r], zero, zero))
        whole = lax.psum(whole, "ctx")
        return jnp.concatenate([lax.dynamic_index_in_dim(whole, other_u[r], 0, False) for r in range(C)], axis=1)

    zero = jnp.uint32(0)
    where = {d: i for i, d in enumerate(exp_walk)}
    left_table = [[exp_walk[(where[i] - s) % E] for s in range(E)] for i in range(E)]
    left_now = lax.dynamic_index_in_dim(jnp.array(left_table, jnp.uint32), e.astype(jnp.uint32), 0, False)
    left_of = [left_now[s] for s in range(E)]

    def put_rows(blocks):
        full = jnp.zeros((E, *blocks[0].shape), BF)
        for s in range(E):
            full = lax.dynamic_update_slice(full, blocks[s][None], (left_of[s], zero, zero))
        return full
    ctx_table = [
        [(i // CORES - r // CORES) % Y * CORES + (i % CORES ^ r % CORES) for r in range(C)] for i in range(C)
    ]
    others = lax.dynamic_index_in_dim(jnp.array(ctx_table, jnp.int32), c.astype(jnp.uint32), 0, False)
    other_u = [others[r].astype(jnp.uint32) for r in range(C)]

    T, D = layer_input.shape[1:]
    rows_e = w_query.shape[0]
    cols_c = D // C
    S = T * C
    half = T // 2
    c_col = (c * cols_c).astype(jnp.uint32)
    NE = w_router.shape[1]
    K = routes.shape[2]
    J = w_gate_up.shape[0]
    cap = (5 * T * K + 4 * NE - 1) // (4 * NE)
    room = -(-cap // 16) * 16
    x = layer_input[0]
    grad_out = d_out[0]

    x_blocks = ctx_gather(x)
    x_all = jnp.concatenate(x_blocks, axis=0)

    small = jnp.concatenate([w_router.reshape(-1), norm_gains.reshape(-1), routes.astype(BF).reshape(-1)])
    small_len = small.shape[0]
    small = jnp.pad(small, (0, -small_len % 4096)).reshape(-1, 128)
    w_qkv_mine = jnp.concatenate(
        [lax.dynamic_slice_in_dim(w, c_col, cols_c, axis=1) for w in (w_query, w_key, w_value)], axis=1
    )
    qkv_walk, small_walk = Gather(ring, w_qkv_mine), Gather(ring, small)
    for _ in range(E // 2):
        small_walk.hop()
        qkv_walk.hop()
        if qkv_walk.count == 2:
            qkv_walk.latest = [v + zero_of(x_blocks[-CORES]).astype(BF) for v in qkv_walk.latest]
        small_walk.latest = [after(v, *qkv_walk.latest) for v in small_walk.latest]
    order = [E // 2, 0] + [i for s in range(1, E // 2) for i in (s, E - s)]
    small_all = jnp.stack([small_walk.got[i] for i in order])
    by_owner = put_rows(small_walk.got)
    cut = rows_e * NE // 128, rows_e * (NE + norm_gains.shape[1]) // 128, small_len // 128
    router_full = by_owner[:, : cut[0]].reshape(D, NE)
    gains = by_owner[:, cut[0] : cut[1]].reshape(D, -1).astype(F32).T
    routes_all = small_all[:, cut[1] : cut[2]].reshape(E, T * K)

    def my_columns(w):
        return lax.dynamic_slice_in_dim(w, c_col, cols_c, axis=1)

    qkv_blocks = qkv_walk.got
    w_qkv = put_rows(qkv_blocks).reshape(D, 3 * cols_c)
    qkv_there = qkv_blocks[E // 2]
    w_out_cols = lax.all_gather(my_columns(w_output), "exp", axis=0, tiled=True)
    w_out_rows = lax.all_to_all(w_out_cols.reshape(C, cols_c, cols_c), "ctx", split_axis=0, concat_axis=0, tiled=True)
    w_out_rows = jnp.transpose(w_out_rows, (1, 0, 2)).reshape(cols_c, D)

    d_walk = Gather(ring, after(grad_out, qkv_there))
    d_walk.hop()
    dn_blocks = ctx_gather(w_down)
    w_dn = jnp.concatenate(dn_blocks, axis=2)

    def hold(v, *others):
        return v + zero_of(*others).astype(v.dtype)

    gu_first = ctx_gather(hold(w_gate_up[: J // 2], dn_blocks[-CORES]))

    blocks_rel = jnp.stack([lax.dynamic_slice_in_dim(block_ids[0], other_u[r] * 2, 2) for r in range(C)]).reshape(-1)
    positions = (blocks_rel[:, None] * half + jnp.arange(half, dtype=jnp.int32)[None, :]).reshape(-1)
    count = jnp.arange(2 * C, dtype=jnp.int32)
    place = jnp.sum(jnp.where(blocks_rel[None, :] == count[:, None], count[None, :], 0), axis=1)
    cosine, sine = angle_tables(positions)
    gain_q = lax.dynamic_slice_in_dim(gains[1:2], c_col, cols_c, axis=1)
    gain_k = lax.dynamic_slice_in_dim(gains[2:3], c_col, cols_c, axis=1)

    groups = [([0], 1)] + [([s, E - s], s) for s in range(1, E // 2)] + [([E // 2], 0)]
    first = (e * J).astype(jnp.int32).reshape(1)
    mine = first[0] + jnp.arange(J, dtype=jnp.int32)
    pairs = (routes_all[:, None, :] == mine[None, :, None].astype(BF)).astype(BF).reshape(E * J, T * K)
    token = jnp.arange(T * K)[:, None] // K
    chosen = dot(pairs, (token == jnp.arange(T)[None, :]).astype(BF), ((1,), (0,)))
    rank = dot(pairs, (token < jnp.arange(T)[None, :]).astype(BF), ((1,), (0,)))
    slot = jnp.where((chosen > 0.5) & (rank < cap), rank, -1.0).astype(jnp.int32).reshape(E, J, T)
    slot_row, slot_col = slot[:, :, None, :], slot[:, :, :, None]

    line, d_slots = Line(), {}

    def fetch(g):
        members, at = groups[g]
        d_slots[g] = dispatch(line.tie(slot_row), at, [d_walk.got[i] for i in members], w_dn, room)
        line.mark(d_slots[g][1])

    fetch(0)
    x_all32 = x_all.astype(F32)
    n1 = (x_all32 * inv_rms(x_all32) * gains[0]).astype(BF)
    qkv = dot(n1, w_qkv, ((1,), (0,)))
    qp, kp = qkv[:, :cols_c], qkv[:, cols_c : 2 * cols_c]
    squares = hold(jnp.stack([jnp.sum(qp * qp, axis=1), jnp.sum(kp * kp, axis=1)]), gu_first[-CORES], d_slots[0][1])
    scales = lax.rsqrt(ctx_sum(squares) / D + epsilon)
    r_q, r_k = scales[0][:, None], scales[1][:, None]
    d_walk.latest = [hold(v, scales) for v in d_walk.latest]
    d_walk.hop()
    gu_last = ctx_gather(hold(w_gate_up[J // 2 :], scales))
    w_gu = lax.optimization_barrier(jnp.concatenate([jnp.concatenate(b, axis=2) for b in (gu_first, gu_last)], axis=0))
    attn, q, k, v, lse = attend(place, qkv, r_q, r_k, cosine, sine, gain_q, gain_k, half)
    branch_part = dot(attn, w_out_rows, ((1,), (0,))).astype(BF)
    chips = chip_sums(lambda r: branch_part[r * T : (r + 1) * T])
    branch = y_sum([hold(v, gu_last[-CORES]) for v in chips])
    d_walk.latest = [hold(v, branch_part) for v in d_walk.latest]
    while d_walk.count < E // 2 - 1:
        d_walk.hop()
    line.mark(branch_part)
    fetch(1)
    branch = hold(branch, w_gu[-1:, -1:, -1:], d_slots[1][1])
    hidden = x.astype(F32) + branch
    n2 = (hidden * inv_rms(hidden) * gains[3]).astype(BF)
    router_own = jax.nn.softmax(dot(n2, router_full, ((1,), (0,))), axis=-1)
    router_high = router_own.astype(BF)
    router_low = (router_own - router_high.astype(F32)).astype(BF)
    n2_wide = jnp.concatenate([n2, router_high, router_low, jnp.zeros((T, PAD - 2 * NE), BF)], axis=1)

    line, n2_walk, done = Line(), Gather(ring, n2_wide), {}

    def work(g):
        members, at = groups[g]
        done[g] = expert(first, line.tie(slot_row), at, [n2_walk.got[i] for i in members], w_gu, d_slots[g][1], room, NE)
        line.mark(done[g][1])

    def back(g):
        members, at = groups[g]
        _, dg, du, _, dgate = done[g]
        kind = F32 if members == [0] else BF
        got = combine(slot_col, at, [(dg, w_gu, 0), (du, w_gu, 1)], room, [None] * len(members), line.tie(first), dgate, NE, out_dtype=kind)
        line.mark(got[0])
        return got

    def mix(g):
        members, at = groups[g]
        kind = F32 if members == [0] else BF
        got = combine(slot_col, at, [(done[g][3], w_dn, 0)], room, [None] * len(members), line.tie(first), out_dtype=kind)
        line.mark(got[0])
        return got

    def grads(left, right):
        parts = wgrad(line.zero(), left, right, C)
        line.mark(parts[0])
        return chip_sums(lambda r: parts[r])

    far = E // 2
    n2_walk.hop()
    line.mark(n2_wide)
    work(0)
    d_walk.latest = [hold(v, done[0][1]) for v in d_walk.latest]
    d_walk.hop()
    fetch(2)
    for g in range(1, far + 1):
        line.mark(*n2_walk.latest, line.last[0])
        if g < far:
            n2_walk.hop()
        work(g)
        if g + 1 < far:
            fetch(g + 2)
    home = Home(ring, back(far)[0])
    for g in range(far - 1, 0, -1):
        terms = back(g)
        line.mark(*home.arrived, line.last[0])
        home.hop(*terms)
    [own] = back(0)
    chips_g = grads([done[i][0] for i in done], [done[i][1] for i in done])
    [mix_far] = mix(far)
    line.mark(*home.arrived, line.last[0])
    rows_back = own + home.arrived[0].astype(F32) + home.arrived[1].astype(F32)
    mixed = Home(ring, after(mix_far, *home.arrived))
    drouter = rows_back[:, D : D + NE] + rows_back[:, D + NE : D + 2 * NE]
    dlogits = (router_own * (drouter - jnp.sum(drouter * router_own, axis=-1, keepdims=True))).astype(BF)
    dn2 = rows_back[:, :D] + dot(dlogits, router_full, ((1,), (1,)))
    hidden_part, d_gain3 = norm_back(hidden, gains[3], dn2)
    dhidden = grad_out.astype(F32) + hidden_part
    dhidden_low = dhidden.astype(BF)
    dhidden_blocks = ctx_gather(dhidden_low)
    dhidden_all = jnp.concatenate(dhidden_blocks, axis=0)
    line.mark(dhidden_low)
    terms = {}
    for g in range(far - 1, -1, -1):
        terms[g] = mix(g)
        if g == far - 1:
            line.mark(*mixed.arrived, line.last[0])
            mixed.hop(*terms[g])
            line.mark(*terms[g])
            chips_u = grads([done[i][0] for i in done], [done[i][2] for i in done])
    sum_g = y_sum([hold(v, dhidden_blocks[-CORES]) for v in chips_g])

    def pump():
        if mixed.near > 1:
            line.mark(*mixed.arrived, *line.last)
            mixed.hop(*terms[mixed.near - 1])

    dattn = dot(after(dhidden_all, *line.last), w_out_rows, ((1,), (1,))).astype(BF)
    g_out = dot(attn, dhidden_all, ((0,), (0,))).astype(BF)
    line.mark(g_out, dattn)
    pump()
    wq, wk, dv, inside, d_gain_qk = attend_back(line.tie(place), q, k, v, dattn, lse, qkv, r_q, r_k, cosine, sine, gain_q, gain_k, half)
    line.mark(dv)
    pump()
    def next_hop(walk, of):
        if walk.near > 1:
            line.mark(*walk.arrived, *line.last)
            walk.hop(of(walk.near - 1), of(E - walk.near + 1))

    g_out = jnp.transpose(g_out.reshape(cols_c, C, cols_c), (1, 0, 2))
    g_out = lax.all_to_all(g_out, "ctx", split_axis=0, concat_axis=0, tiled=True).reshape(E, rows_e, cols_c)
    g_router = dot(dlogits, n2, ((0,), (0,)))
    spread = lax.dynamic_update_slice(jnp.zeros((2, D), F32), d_gain_qk, (zero, c_col))
    g_small = jnp.concatenate([g_router, spread, d_gain3[None]], axis=0)
    count = g_small.shape[0]
    g_small = jnp.transpose(g_small.reshape(count, E, rows_e), (1, 0, 2)).reshape(E, -1)
    unit = 3 * 16
    small_rows = -(-(rows_e * cols_c + count * rows_e) // (cols_c * unit)) * unit - rows_e
    g_small = jnp.pad(g_small, ((0, 0), (0, small_rows * cols_c - count * rows_e))).reshape(E, small_rows, cols_c)
    more = jnp.concatenate([g_out, g_small.astype(BF)], axis=1).reshape(E, -1, 3 * cols_c)
    more = lax.optimization_barrier(more)

    inside = ctx_sum(hold(line.tie(inside)[:, :2].T, sum_g, more)) / D
    dqp = r_q * wq - qp * (r_q * r_q * r_q * inside[0][:, None])
    dkp = r_k * wk - kp * (r_k * r_k * r_k * inside[1][:, None])
    dqkv = jnp.concatenate([dqp.astype(BF), dkp.astype(BF), dv], axis=1)
    g_qkv = dot(n1, dqkv, ((0,), (0,))).astype(BF).reshape(E, rows_e, 3 * cols_c)

    def of_qkv(s):
        return jnp.concatenate([lax.dynamic_index_in_dim(a, left_of[s], 0, False) for a in (g_qkv, more)], axis=0)

    qkv_home = Home(ring, of_qkv(far))
    sum_u = y_sum([hold(v, inside) for v in chips_u])
    line.mark(g_qkv)
    dn1_part = dot(line.tie(dqkv), w_qkv, ((1,), (1,))).astype(BF)
    line.mark(dn1_part)
    next_hop(qkv_home, lambda s: hold(of_qkv(s), sum_u))
    chips_n1 = chip_sums(lambda r: dn1_part[r * T : (r + 1) * T])
    dn1 = y_sum(chips_n1)
    next_hop(qkv_home, of_qkv)
    line.mark(*qkv_home.sent, *mixed.arrived)
    chips_d = grads([d_slots[i][0] for i in done], [done[i][3] for i in done])
    sum_d = y_sum(chips_d)

    def arrived_sum(walk, own):
        return own.astype(F32) + walk.arrived[0].astype(F32) + walk.arrived[1].astype(F32)

    while qkv_home.near > 1:
        next_hop(qkv_home, lambda s: hold(of_qkv(s), sum_d))
    x32 = x.astype(F32)
    token_part, _ = norm_back(x32, gains[0], dn1)
    d_x = (dhidden + token_part)[None]
    g_gate_up = jnp.concatenate([sum_g, sum_u], axis=1)
    g_down = sum_d
    while mixed.near > 1:
        pump()
    output = (hidden + terms[0][0] + mixed.arrived[0].astype(F32) + mixed.arrived[1].astype(F32)).astype(BF)[None]

    dense_mine = arrived_sum(qkv_home, of_qkv(0))
    g_qkv_mine = dense_mine[:rows_e]
    own_gain = norm_gains[:, 0].astype(F32)
    d_gain0 = jnp.sum(w_qkv_mine.astype(F32) * g_qkv_mine, axis=1) / own_gain
    gain_rows = -(-rows_e // (3 * cols_c * 16)) * 16
    d_gain0 = jnp.pad(d_gain0, (0, gain_rows * 3 * cols_c - rows_e)).reshape(gain_rows, 3 * cols_c)
    pieces = ctx_gather(jnp.concatenate([dense_mine, d_gain0], axis=0).astype(BF))
    g_query, g_key, g_value = columns(others, pieces, rows_e, cols_c)
    last = dense_mine.shape[0]
    out_pieces = [p[rows_e:last].reshape(-1, cols_c) for p in pieces]
    [g_output] = columns(others, out_pieces, rows_e, cols_c)
    g_small = sum(p[rows_e:].astype(F32) for p in out_pieces).reshape(-1)[: count * rows_e].reshape(count, rows_e)
    d_gain0 = sum(p[last:].astype(F32) for p in pieces).reshape(-1)[:rows_e]
    g_gains = jnp.concatenate([d_gain0[None], g_small[NE:]], axis=0).T
    return (output, d_x, g_query, g_key, g_value, g_output, g_small[:NE].T, g_gains, g_gate_up, g_down)


def solution(mesh):
    exp_walk = ring_order(mesh.shape["exp"])
    tokens = P("exp", "ctx", None)
    rows = P("exp", None)
    hidden_units = P("exp", None, "ctx")
    in_specs = (tokens, rows, tokens) + (rows,) * 6 + (hidden_units, hidden_units, tokens)
    out_specs = (tokens, tokens) + (rows,) * 6 + (hidden_units, hidden_units)
    return jax.shard_map(
        functools.partial(per_device, exp_walk),
        mesh=mesh,
        in_specs=in_specs,
        out_specs=out_specs,
        check_vma=False,
    )
```
